128 devices in a mesh: grp: 4 (over z), work: 32 (over y, x, core).
Axes of the slice: x: 4, y: 4, z: 4, core: 2. Of those that a mesh axis runs over, the one named last changes fastest.
Arguments:
- embeddings: bfloat16 [131072, 1024], P(('grp', 'work')), may hold values from -250 to 250
- offsets: int32 [257], replicated, may hold values from 0 to 131072, as said below
Outputs:
- best_match: float32 [131072], P(('grp', 'work'))
The draws below stay inside these ranges and needn't reach their ends.
Inputs may be any that keep to these rules, and one draw needn't show every extreme that they name: offsets[0] is 0 and each later entry exceeds the one before by 512 to 6144 rows, by exactly 6144 at least once, except that the last cluster may be shorter so as to end at 131072; all entries after it equal 131072. Cluster c holds rows offsets[c] up to offsets[c+1] - 1.
All inputs are finite; a program needn't handle non-finite values.
Results may differ from the reference program's by a relative error of at most 0.00048.
Values may be sent and summed in bfloat16 or wider, within the bound.
A program may use at most 64 MiB of HBM per device.

```python
import math
import jax
import jax.numpy as jnp
from jax import lax

D = 1024
MOST = 6144
MIN_C = 512
ROWS = 131072
CLUSTER_CAP = 256


def make_offsets(key):
    base_key = jax.random.fold_in(key, 7331)
    key_sizes, key_place = jax.random.split(base_key)
    cluster_sizes = jax.random.randint(key_sizes, (CLUSTER_CAP,), MIN_C, MOST + 1)
    chosen = jax.random.randint(key_place, (), 0, ROWS // MOST)
    cluster_sizes = jnp.where(jnp.arange(CLUSTER_CAP) == chosen, MOST, cluster_sizes)
    cumulative = jnp.minimum(jnp.cumsum(cluster_sizes), ROWS).astype(jnp.int32)
    return jnp.concatenate([jnp.zeros((1,), jnp.int32), cumulative])


def draw_offsets(key, part):
    return make_offsets(key)


def draw_embeddings(key, part):
    offset_table = make_offsets(key)
    row_index = jnp.arange(ROWS, dtype=jnp.int32)
    cluster_ids = jnp.searchsorted(offset_table[1:], row_index, side='right').astype(jnp.int32)
    cluster_ids = jnp.minimum(cluster_ids, CLUSTER_CAP - 1)
    cluster_starts = offset_table[cluster_ids]
    cluster_ends = offset_table[cluster_ids + 1]
    base_key = jax.random.fold_in(key, 99)
    keys_all = jax.random.split(base_key, 8)
    key_center, key_weight, key_noise, key_scale = (keys_all[0], keys_all[1], keys_all[2], keys_all[3])
    key_pick, key_partner, key_close = (keys_all[5], keys_all[6], keys_all[7])
    centroid = jnp.clip(jax.random.normal(key_center, (CLUSTER_CAP, D), jnp.float32), -6.0, 6.0)
    weight = jnp.exp(jax.random.uniform(key_weight, (CLUSTER_CAP,), jnp.float32, math.log(0.3), math.log(3.0)))
    row_scale = jnp.exp(jax.random.uniform(key_scale, (ROWS, 1), jnp.float32, 0.0, math.log(10.0)))
    noise_part = jnp.clip(jax.random.normal(key_noise, (ROWS, D), jnp.float32), -6.0, 6.0)
    is_copy = jax.random.randint(key_pick, (ROWS,), 0, 20) == 0
    partner = jax.random.randint(key_partner, (ROWS,), cluster_starts, cluster_ends).astype(jnp.int32)
    cluster_width = jnp.maximum(cluster_ends - cluster_starts, 1)
    partner = jnp.where(partner == row_index, cluster_starts + (row_index - cluster_starts + 1) % cluster_width, partner)
    close_noise = jnp.clip(jax.random.normal(key_close, (ROWS, D), jnp.float32), -3.0, 3.0)
    copied = noise_part[partner] + 0.02 * close_noise
    noise_part = jnp.where(is_copy[:, None], copied, noise_part)
    values = row_scale * (weight[cluster_ids][:, None] * centroid[cluster_ids] + noise_part)
    return values.astype(jnp.bfloat16)


def setup_inputs(seed: int = 0) -> dict:
    keys = jax.random.split(jax.random.key(seed), 3)
    embeddings = draw_embeddings(jax.random.fold_in(keys[2], 71), 0)
    offsets = draw_offsets(jax.random.fold_in(keys[2], 71), 0)
    return dict(embeddings=embeddings, offsets=offsets)


def to_unit(values):
    widened = values.astype(jnp.float32)
    factor = lax.rsqrt(lax.optimization_barrier(jnp.mean(widened * widened, axis=1, keepdims=True)) + 1e-06) / math.sqrt(values.shape[1])
    return (widened * factor).astype(jnp.bfloat16)

def reference(embeddings, offsets):
    unit_rows = to_unit(embeddings)
    row_index = jnp.arange(ROWS, dtype=jnp.int32)
    cluster_ids = jnp.searchsorted(offsets[1:], row_index, side='right').astype(jnp.int32)
    margin_rows = jnp.zeros((MOST, D), jnp.bfloat16)
    padded_rows = jnp.concatenate([margin_rows, unit_rows, margin_rows], axis=0)
    margin_ids = jnp.full((MOST,), -2, jnp.int32)
    padded_ids = jnp.concatenate([margin_ids, cluster_ids, margin_ids], axis=0)
    block_rows = math.gcd(512, ROWS)
    window = block_rows + 2 * MOST

    def one_block(block_index):
        first_row = (block_index * block_rows).astype(jnp.int32)
        left_rows = lax.dynamic_slice(unit_rows, (first_row, jnp.int32(0)), (block_rows, D))
        left_ids = lax.dynamic_slice(cluster_ids, (first_row,), (block_rows,))
        right_rows = lax.dynamic_slice(padded_rows, (first_row, jnp.int32(0)), (window, D))
        right_ids = lax.dynamic_slice(padded_ids, (first_row,), (window,))
        scores = jnp.dot(left_rows, right_rows.T, preferred_element_type=jnp.float32)
        left_global = first_row + jnp.arange(block_rows, dtype=jnp.int32)
        right_global = first_row - MOST + jnp.arange(window, dtype=jnp.int32)
        same_cluster = (left_ids[:, None] == right_ids[None, :]) & (left_global[:, None] != right_global[None, :])
        masked = jnp.where(same_cluster, scores, jnp.full(scores.shape, -1.0, scores.dtype))
        return lax.optimization_barrier(jnp.max(masked, axis=1))
    blocks = lax.map(one_block, jnp.arange(ROWS // block_rows, dtype=jnp.int32))
    return blocks.reshape(ROWS)
```

```python
import math

import jax
import jax.numpy as jnp
from jax import lax
from jax.sharding import PartitionSpec as P

AXES = ("grp", "work")


def permuted(block, target):
    count = lax.axis_size(AXES)
    return lax.ppermute(block, AXES, [(i, target(i) % count) for i in range(count)])


def to_unit(values):
    widened = values.astype(jnp.float32)
    factor = lax.rsqrt(jnp.mean(widened * widened, axis=1, keepdims=True) + 1e-06) / math.sqrt(
        values.shape[1]
    )
    return (widened * factor).astype(jnp.bfloat16)


def cluster_of(offsets, first_row, row_count):
    row_index = first_row + jnp.arange(row_count, dtype=jnp.int32)
    return jnp.sum((offsets[None, 1:] <= row_index[:, None]).astype(jnp.int32), axis=1)


def pair_tile(left_rows, right_rows, left_ids, right_ids, same_block=False):
    scores = lax.dot_general(
        left_rows, right_rows, (((1,), (1,)), ((), ())), preferred_element_type=jnp.float32
    )
    same_cluster = left_ids[:, None] == right_ids[None, :]
    if same_block:
        positions = jnp.arange(left_ids.shape[0], dtype=jnp.int32)
        same_cluster = same_cluster & (positions[:, None] != positions[None, :])
    masked = jnp.where(same_cluster, scores, -1.0)
    return (jnp.max(masked, axis=1), jnp.max(masked, axis=0))


def shards(embeddings, offsets):
    row_count = embeddings.shape[0]
    count = lax.axis_size(AXES)
    me = lax.axis_index(AXES)
    core = me % 2

    def ids_of(device):
        return cluster_of(offsets, (device % count) * row_count, row_count)

    own = to_unit(embeddings)
    near = permuted(own, lambda i: i - 2)
    far = permuted(own, lambda i: i - 6)
    near_other = permuted(near, lambda i: i ^ 1)
    extra = permuted(jnp.where(core == 1, own, far), lambda i: i ^ 1)
    other = me + 1 - 2 * core
    own_ids, near_ids, far_ids = ids_of(me), ids_of(me + 2), ids_of(me + 6)
    near_other_ids = ids_of(other + 2)
    extra_ids = ids_of(jnp.where(core == 1, other + 6, other))

    best = pair_tile(own, own, own_ids, own_ids, True)[0]
    row, near_best = pair_tile(own, near, own_ids, near_ids)
    best = jnp.maximum(best, row)
    row, far_best = pair_tile(own, far, own_ids, far_ids)
    best = jnp.maximum(best, row)
    row, near_other_best = pair_tile(own, near_other, own_ids, near_other_ids)
    best = jnp.maximum(best, row)
    row, extra_best = pair_tile(own, extra, own_ids, extra_ids)
    best = jnp.maximum(best, row)
    row, column = pair_tile(far, near, far_ids, near_ids)
    far_best, near_best = jnp.maximum(far_best, row), jnp.maximum(near_best, column)
    row, column = pair_tile(far, near_other, far_ids, near_other_ids)
    far_best, near_other_best = jnp.maximum(far_best, row), jnp.maximum(near_other_best, column)
    best = jnp.maximum(best, permuted(near_best, lambda i: i + 2))
    best = jnp.maximum(best, permuted(near_other_best, lambda i: (i ^ 1) + 2))
    best = jnp.maximum(best, permuted(far_best, lambda i: i + 6))
    best = jnp.maximum(best, permuted(extra_best, lambda i: i + 1 if i % 2 == 0 else i + 5))
    return best


def solution(mesh):
    return jax.shard_map(
        shards,
        mesh=mesh,
        in_specs=(P(AXES, None), P()),
        out_specs=P(AXES),
        check_vma=False,
    )
```

```python
import jax
import jax.numpy as jnp
from jax import lax
from jax.experimental import pallas as pl
from jax.experimental.pallas import tpu as pltpu
from jax.sharding import PartitionSpec as P

AXES = ("grp", "work")
MESH = pl.DeviceIdType.MESH
ROWS = 1024
WIDTH = 1024
STEPS = 8
CHUNK = ROWS // STEPS
PIECES = 4
PIECE = CHUNK // PIECES
CHIPS = 64
DEVICES = 2 * CHIPS
LANES = 128


def dot(left, right):
    return lax.dot_general(
        left, right, (((1,), (1,)), ((), ())), preferred_element_type=jnp.float32
    )


def kernel(
    emb, offs, out,
    raw, own, relay, near, far,
    id_own, id_far, lane_own, lane_near, lane_far, table,
    row_own, row_far, col_near, col_far, reply, heard,
    raw_sem, near_s, far_s, hop_s, swap_s, extra_s, reply_s,
    relay_r, near_r, swap_r, far_r, extra_r, reply_r,
):
    grp = lax.axis_index("grp")
    work = lax.axis_index("work")
    core = work % 2
    x = (work // 2) % 4
    chip = grp * 16 + work // 2
    me = chip * 2 + core

    def device(distance, which):
        target = (chip + distance + CHIPS) % CHIPS
        return (target // 16, (target % 16) * 2 + which)

    partner = device(0, 1 - core)

    def remote(src, dst, send, recv, target):
        return pltpu.make_async_remote_copy(
            src_ref=src, dst_ref=dst, send_sem=send, recv_sem=recv,
            device_id=target, device_id_type=MESH,
        )

    barrier = pltpu.get_barrier_semaphore()

    def greet(target):
        pl.semaphore_signal(barrier, inc=1, device_id=target, device_id_type=MESH)

    greet(partner)
    greet(device(3, core))
    pl.when(x < 3)(lambda: greet(device(1, core)))
    pl.when(x == 3)(lambda: greet(device(-3, core)))
    pl.when(x == 0)(lambda: greet(device(4, core)))

    load = pltpu.make_async_copy(emb, raw, raw_sem)
    load.start()

    for half in range(2):
        part = offs[0:1, half * LANES:(half + 1) * LANES].astype(jnp.float32)
        table[half * LANES:(half + 1) * LANES, :] = jnp.broadcast_to(part, (LANES, LANES)).T

    def lane_ids(owner, group):
        first = (owner % DEVICES) * ROWS + group * LANES
        index = first + lax.broadcasted_iota(jnp.int32, (1, LANES), 1)
        hit = table[...] <= index.astype(jnp.float32)
        return jnp.sum(jnp.where(hit, 1.0, 0.0), axis=0, keepdims=True)

    extra_owner = jnp.where(core == 0, me + 1, me + 5)

    def fill_ids(group, _):
        rows = pl.ds(pl.multiple_of(group * LANES, LANES), LANES)
        mine = lane_ids(me, group)
        lane_own[group] = mine
        id_own[rows, :] = jnp.broadcast_to(mine, (LANES, LANES)).T
        away = lane_ids(me + 6, group)
        id_far[rows, :] = jnp.broadcast_to(away, (LANES, LANES)).T
        lane_far[group, :, 0:LANES] = away
        lane_far[group, :, LANES:2 * LANES] = lane_ids(extra_owner, group)
        lane_near[group, :, 0:LANES] = lane_ids(me + 2, group)
        lane_near[group, :, LANES:2 * LANES] = lane_ids(me + 3 - 2 * core, group)
        return 0

    lax.fori_loop(0, STEPS, fill_ids, 0)
    row_own[...] = jnp.full_like(row_own, -1.0)
    row_far[...] = jnp.full_like(row_far, -1.0)
    col_near[...] = jnp.full_like(col_near, -1.0)
    col_far[...] = jnp.full_like(col_far, -1.0)

    load.wait()

    def normalize(step, _):
        rows = pl.ds(pl.multiple_of(step * CHUNK, CHUNK), CHUNK)
        wide = raw[rows, :].astype(jnp.float32)
        mean = jnp.sum(wide * wide, axis=1, keepdims=True) * (1.0 / WIDTH)
        factor = lax.rsqrt(mean + 1e-06) * (1.0 / 32.0)
        own[rows, :] = (wide * factor).astype(jnp.bfloat16)
        return 0

    lax.fori_loop(0, STEPS, normalize, 0)

    @pl.when(x == 0)
    def _():
        pl.semaphore_wait(barrier, 4)

    @pl.when(x != 0)
    def _():
        pl.semaphore_wait(barrier, 3)

    def chunk(step):
        return own.at[pl.ds(pl.multiple_of(step * CHUNK, CHUNK), CHUNK)]

    def piece(step, part):
        return pl.ds(pl.multiple_of(step * CHUNK + part * PIECE, PIECE), PIECE)

    def near_copy(step):
        return remote(
            chunk(step), near.at[step, 0:CHUNK], near_s.at[step], near_r.at[step], device(-1, core)
        )

    def hop_copy(step, part):
        return remote(
            own.at[piece(step, part)], relay.at[piece(step, part)],
            near_s.at[step], relay_r.at[step, part], device(-4, core),
        )

    def pass_copy(step, part):
        return remote(
            relay.at[piece(step, part)], near.at[step, part * PIECE:(part + 1) * PIECE],
            hop_s.at[step], near_r.at[step], device(3, core),
        )

    def far_copy(step):
        return remote(
            chunk(step), far.at[step, 0:CHUNK], far_s.at[step], far_r.at[step], device(-3, core)
        )

    def swap_copy(step):
        return remote(
            near.at[step, 0:CHUNK], near.at[step, CHUNK:2 * CHUNK],
            swap_s.at[step], swap_r.at[step], partner,
        )

    def extra_own(step):
        return remote(
            chunk(step), far.at[step, CHUNK:2 * CHUNK], extra_s.at[step], extra_r.at[step], partner
        )

    def extra_far(step):
        return remote(
            far.at[step, 0:CHUNK], far.at[step, CHUNK:2 * CHUNK],
            extra_s.at[step], extra_r.at[step], partner,
        )

    def send(step, _):
        @pl.when(x != 0)
        def _():
            near_copy(step).start()

        @pl.when(x == 0)
        def _():
            for part in range(PIECES):
                hop_copy(step, part).start()

        far_copy(step).start()
        pl.when(core == 1)(lambda: extra_own(step).start())
        return 0

    lax.fori_loop(0, STEPS, send, 0)

    def fold(scores, ids, lanes, carried, column, other=None):
        width = scores.shape[1] // LANES
        for j in range(width):
            part = scores[:, j * LANES:(j + 1) * LANES]
            same = ids == lanes[:, j * LANES:(j + 1) * LANES]
            if other is not None:
                same = same & other[j]
            part = jnp.where(same, part, -1.0)
            carried = jnp.maximum(carried, part)
            if column is not None:
                column(j, jnp.max(part.reshape(part.shape[0] // 8, 8, LANES), axis=0))
        return carried

    def raise_to(ref, index):
        def update(j, value):
            at = (index, slice(None), slice(j * LANES, (j + 1) * LANES))
            ref[at] = jnp.maximum(ref[at], value)
        return update

    def diagonal(block, _):
        columns = pl.ds(pl.multiple_of(block * 2 * LANES, 2 * LANES), 2 * LANES)
        scores = dot(own[...], own[columns, :])
        rows = lax.broadcasted_iota(jnp.int32, (ROWS, LANES), 0)
        lanes = lax.broadcasted_iota(jnp.int32, (ROWS, LANES), 1) + block * 2 * LANES
        best = row_own[...]
        for j in range(2):
            part = scores[:, j * LANES:(j + 1) * LANES]
            same = (id_own[...] == lane_own[block * 2 + j]) & (rows != lanes + j * LANES)
            best = jnp.maximum(best, jnp.where(same, part, -1.0))
        row_own[...] = best
        return 0

    lax.fori_loop(0, ROWS // (2 * LANES), diagonal, 0)

    def far_block(first, count, step):
        left = far[pl.ds(first, count), 0:CHUNK, :].reshape(count * CHUNK, WIDTH)
        rows = pl.ds(pl.multiple_of(first * CHUNK, CHUNK), count * CHUNK)
        scores = dot(left, near[step])
        row_far[rows, :] = fold(
            scores, id_far[rows, :], lane_near[step], row_far[rows, :], raise_to(col_near, step)
        )

    def advance(step, _):
        @pl.when(x == 0)
        def _():
            for part in range(PIECES):
                hop_copy(step, part).wait_recv()
                pass_copy(step, part).start()

        near_copy(step).wait_recv()
        swap_copy(step).start()
        far_copy(step).wait_recv()
        pl.when(core == 0)(lambda: extra_far(step).start())
        extra_own(step).wait_recv()
        scores = dot(own[...], far[step])
        row_own[...] = fold(scores, id_own[...], lane_far[step], row_own[...], raise_to(col_far, step))
        swap_copy(step).wait_recv()
        scores = dot(own[...], near[step])
        row_own[...] = fold(scores, id_own[...], lane_near[step], row_own[...], raise_to(col_near, step))

        @pl.when((step % 2 == 1) & (step < STEPS - 1))
        def _():
            def fresh(other, _):
                far_block(step - 1, 2, other)
                return 0

            lax.fori_loop(0, step + 1, fresh, 0)

            def older(pair, _):
                far_block((pair // 2) * 2, 2, step - 1 + pair % 2)
                return 0

            lax.fori_loop(0, step - 1, older, 0)

        @pl.when(step == STEPS - 2)
        def _():
            far_block(0, STEPS - 2, step)

        return 0

    lax.fori_loop(0, STEPS, advance, 0)
    far_block(0, STEPS, STEPS - 1)

    def last(other, _):
        far_block(STEPS - 2, 2, other)
        return 0

    lax.fori_loop(0, STEPS - 1, last, 0)

    def flat(ref):
        return jnp.concatenate(
            [
                jnp.max(ref[g * LANES:(g + 1) * LANES, :].T, axis=0, keepdims=True)
                for g in range(STEPS)
            ],
            axis=0,
        )

    best_near = jnp.max(col_near[...], axis=1)
    best_far = jnp.max(col_far[...], axis=1)
    reply[0] = best_near[:, 0:LANES]
    reply[1] = best_near[:, LANES:2 * LANES]
    reply[2] = jnp.maximum(best_far[:, 0:LANES], flat(row_far))
    reply[3] = best_far[:, LANES:2 * LANES]

    def answer(slot, target):
        return remote(reply.at[slot], heard.at[slot], reply_s.at[slot], reply_r.at[slot], target)

    answer(2, device(3, core)).start()
    pl.when(core == 0)(lambda: answer(3, partner).start())
    pl.when(core == 1)(lambda: answer(3, device(3, 0)).start())
    answer(0, device(1, core)).start()
    answer(1, device(1, 1 - core)).start()
    best = flat(row_own)
    for slot in range(4):
        answer(slot, partner).wait_recv()
        best = jnp.maximum(best, heard[slot])
    out[...] = best

    def drain(step, _):
        near_copy(step).wait_send()
        far_copy(step).wait_send()
        swap_copy(step).wait_send()
        extra_own(step).wait_send()

        @pl.when(x == 0)
        def _():
            remote(
                chunk(step), near.at[step, 0:CHUNK], hop_s.at[step], near_r.at[step], partner
            ).wait_send()

        return 0

    lax.fori_loop(0, STEPS, drain, 0)
    for slot in range(4):
        answer(slot, partner).wait_send()


def shards(embeddings, offsets):
    block = pltpu.VMEM((ROWS, WIDTH), jnp.bfloat16)
    wide = pltpu.VMEM((ROWS, LANES), jnp.float32)
    steps = pltpu.SemaphoreType.DMA((STEPS,))
    best = pl.pallas_call(
        kernel,
        out_shape=jax.ShapeDtypeStruct((STEPS, LANES), jnp.float32),
        in_specs=[
            pl.BlockSpec(memory_space=pl.ANY),
            pl.BlockSpec(memory_space=pltpu.VMEM),
        ],
        out_specs=pl.BlockSpec(memory_space=pltpu.VMEM),
        scratch_shapes=[
            block, block, block,
            pltpu.VMEM((STEPS, 2 * CHUNK, WIDTH), jnp.bfloat16),
            pltpu.VMEM((STEPS, 2 * CHUNK, WIDTH), jnp.bfloat16),
            wide, wide,
            pltpu.VMEM((STEPS, 1, LANES), jnp.float32),
            pltpu.VMEM((STEPS, 1, 2 * LANES), jnp.float32),
            pltpu.VMEM((STEPS, 1, 2 * LANES), jnp.float32),
            pltpu.VMEM((2 * LANES, LANES), jnp.float32),
            wide, wide,
            pltpu.VMEM((STEPS, 8, 2 * LANES), jnp.float32),
            pltpu.VMEM((STEPS, 8, 2 * LANES), jnp.float32),
            pltpu.VMEM((4, STEPS, LANES), jnp.float32),
            pltpu.VMEM((4, STEPS, LANES), jnp.float32),
            pltpu.SemaphoreType.DMA(()),
            steps, steps, steps, steps, steps, pltpu.SemaphoreType.DMA((4,)),
            pltpu.SemaphoreType.DMA((STEPS, PIECES)),
            steps, steps, steps, steps, pltpu.SemaphoreType.DMA((4,)),
        ],
        compiler_params=pltpu.CompilerParams(
            collective_id=0, has_side_effects=True, vmem_limit_bytes=62 * 1024 * 1024
        ),
        name="match",
    )(embeddings, offsets.reshape(1, -1))
    return best.reshape(-1)


def solution(mesh):
    return jax.shard_map(
        shards,
        mesh=mesh,
        in_specs=(P(AXES, None), P()),
        out_specs=P(AXES),
        check_vma=False,
    )
```

```python
import functools

import jax
import jax.numpy as jnp
from jax import lax
from jax.experimental import pallas as pl
from jax.experimental.pallas import tpu as pltpu
from jax.sharding import PartitionSpec as P

AXES = ("grp", "work")
MESH = pl.DeviceIdType.MESH
ROWS = 1024
WIDTH = 1024
STEPS = 8
CHUNK = ROWS // STEPS
PIECES = 4
PIECE = CHUNK // PIECES
CHIPS = 64
DEVICES = 2 * CHIPS
LANES = 128


def dot(left, right):
    return lax.dot_general(
        left, right, (((1,), (1,)), ((), ())), preferred_element_type=jnp.float32
    )


def kernel(
    emb, offs, out,
    raw, own, relay, gathered,
    id_own, id_rows, lane_own, lane_ids, table, row_own, columns, reply, heard,
    raw_sem, near_s, far_s, hop_s, swap_s, extra_s, reply_s,
    relay_r, near_r, swap_r, far_r, extra_r, reply_r,
):
    grp = lax.axis_index("grp")
    work = lax.axis_index("work")
    core = work % 2
    x = (work // 2) % 4
    chip = grp * 16 + work // 2
    me = chip * 2 + core

    def device(distance, which):
        target = (chip + distance + CHIPS) % CHIPS
        return (target // 16, (target % 16) * 2 + which)

    partner = device(0, 1 - core)

    def remote(src, dst, send, recv, target):
        return pltpu.make_async_remote_copy(
            src_ref=src, dst_ref=dst, send_sem=send, recv_sem=recv,
            device_id=target, device_id_type=MESH,
        )

    barrier = pltpu.get_barrier_semaphore()

    def greet(target):
        pl.semaphore_signal(barrier, inc=1, device_id=target, device_id_type=MESH)

    greet(device(3, core))
    pl.when(x == 0)(lambda: greet(device(4, core)))
    pl.when(x < 3)(lambda: greet(device(1, core)))
    pl.when(x == 3)(lambda: greet(device(-3, core)))
    greet(partner)

    def chunk_rows(step):
        return pl.ds(pl.multiple_of(step * CHUNK, CHUNK), CHUNK)

    def chunk(step):
        return own.at[chunk_rows(step)]

    def load(step):
        return pltpu.make_async_copy(
            emb.at[chunk_rows(step)], raw.at[chunk_rows(step)], raw_sem.at[step]
        )

    for step in range(STEPS):
        load(step).start()

    def normalize(step):
        load(step).wait()
        rows = chunk_rows(step)
        wide = raw[rows, :].astype(jnp.float32)
        mean = jnp.sum(wide * wide, axis=1, keepdims=True) * (1.0 / WIDTH)
        factor = lax.rsqrt(mean + 1e-06) * (1.0 / 32.0)
        own[rows, :] = (wide * factor).astype(jnp.bfloat16)

    def piece(step, part):
        return pl.ds(pl.multiple_of(step * CHUNK + part * PIECE, PIECE), PIECE)

    def slot(step, kind):
        return gathered.at[step, kind * CHUNK:(kind + 1) * CHUNK]

    def near_copy(step):
        return remote(
            chunk(step), slot(step, 0), near_s.at[step], near_r.at[step], device(-1, core)
        )

    def hop_copy(step, part):
        return remote(
            own.at[piece(step, part)], relay.at[piece(step, part)],
            near_s.at[step], relay_r.at[step, part], device(-4, core),
        )

    def pass_copy(step, part):
        return remote(
            relay.at[piece(step, part)], gathered.at[step, part * PIECE:(part + 1) * PIECE],
            hop_s.at[step], near_r.at[step], device(3, core),
        )

    def far_copy(step):
        return remote(
            chunk(step), slot(step, 2), far_s.at[step], far_r.at[step], device(-3, core)
        )

    def swap_copy(step):
        return remote(slot(step, 0), slot(step, 1), swap_s.at[step], swap_r.at[step], partner)

    def extra_own(step):
        return remote(chunk(step), slot(step, 3), extra_s.at[step], extra_r.at[step], partner)

    def extra_far(step):
        return remote(slot(step, 2), slot(step, 3), extra_s.at[step], extra_r.at[step], partner)

    def send(step):
        far_copy(step).start()

        @pl.when(x != 0)
        def _():
            near_copy(step).start()

        @pl.when(x == 0)
        def _():
            for part in range(PIECES):
                hop_copy(step, part).start()

        pl.when(core == 1)(lambda: extra_own(step).start())

    normalize(0)
    normalize(1)

    @pl.when(x == 0)
    def _():
        pl.semaphore_wait(barrier, 4)

    @pl.when(x != 0)
    def _():
        pl.semaphore_wait(barrier, 3)

    send(0)

    def start(step, _):
        normalize(step)
        send(step - 1)
        return 0

    lax.fori_loop(2, STEPS, start, 0)

    def fill_table(index, _):
        table[pl.ds(index, 1), :] = jnp.full((1, LANES), offs[index], jnp.int32)
        return 0

    lax.fori_loop(0, 2 * LANES, fill_table, 0, unroll=8)
    send(STEPS - 1)

    def ids_of(owner, group):
        first = (owner % DEVICES) * ROWS + group * LANES
        index = first + lax.broadcasted_iota(jnp.int32, (1, LANES), 1)
        return jnp.sum(jnp.where(table[...] <= index, 1.0, 0.0), axis=0, keepdims=True)

    extra_owner = jnp.where(core == 0, me + 1, me + 5)

    def fill_ids(group, _):
        mine = ids_of(me, group)
        lane_own[group] = mine
        id_own[chunk_rows(group), :] = jnp.broadcast_to(mine, (LANES, LANES)).T
        owners = (me + 2, me + 3 - 2 * core, me + 6, extra_owner)
        for kind in range(4):
            ids = ids_of(owners[kind], group)
            lane_ids[group, :, kind * LANES:(kind + 1) * LANES] = ids
            if kind < 3:
                id_rows[group, kind * LANES:(kind + 1) * LANES, :] = jnp.broadcast_to(
                    ids, (LANES, LANES)
                ).T
        return 0

    lax.fori_loop(0, STEPS, fill_ids, 0)
    row_own[...] = jnp.full_like(row_own, -1.0)
    columns[...] = jnp.full_like(columns, -1.0)

    def fold(scores, ids, lanes, carried, targets):
        for j in range(len(lanes)):
            part = scores[:, j * LANES:(j + 1) * LANES]
            part = jnp.where(ids == lanes[j], part, -1.0)
            carried = part if carried is None else jnp.maximum(carried, part)
            step, kind = targets[j]
            at = (step, slice(None), slice(kind * LANES, (kind + 1) * LANES))
            best = jnp.max(part.reshape(part.shape[0] // 8, 8, LANES), axis=0)
            columns[at] = jnp.maximum(columns[at], best)
        return carried

    def lanes_of(step, kind):
        return lane_ids[step, :, kind * LANES:(kind + 1) * LANES]

    def turned(rows):
        return jnp.max(rows.T, axis=0, keepdims=True)

    def diagonal(block, _):
        first = pl.multiple_of(block * 2 * LANES, 2 * LANES)
        scores = dot(own[...], own[pl.ds(first, 2 * LANES), :])
        rows = lax.broadcasted_iota(jnp.int32, (ROWS, LANES), 0)
        lanes = lax.broadcasted_iota(jnp.int32, (ROWS, LANES), 1) + first
        best = row_own[...]
        for j in range(2):
            part = scores[:, j * LANES:(j + 1) * LANES]
            same = (id_own[...] == lane_own[block * 2 + j]) & (rows != lanes + j * LANES)
            best = jnp.maximum(best, jnp.where(same, part, -1.0))
        row_own[...] = best
        return 0

    lax.fori_loop(0, ROWS // (2 * LANES), diagonal, 0)

    def older(step):
        right = gathered[0:step, 0:2 * CHUNK, :].reshape(step * 2 * CHUNK, WIDTH)
        scores = dot(gathered[step, 2 * CHUNK:3 * CHUNK, :], right)
        pairs = [(s, kind) for s in range(step) for kind in range(2)]
        best = fold(
            scores, id_rows[step, 2 * CHUNK:3 * CHUNK, :],
            [lanes_of(s, kind) for s, kind in pairs], None, pairs,
        )
        at = (step, slice(0, 1), slice(2 * LANES, 3 * LANES))
        columns[at] = jnp.maximum(columns[at], turned(best))

    def newer(step):
        right = gathered[0:step + 1, 2 * CHUNK:3 * CHUNK, :].reshape((step + 1) * CHUNK, WIDTH)
        scores = dot(gathered[step, 0:2 * CHUNK, :], right)
        pairs = [(s, 2) for s in range(step + 1)]
        best = fold(
            scores, id_rows[step, 0:2 * CHUNK, :],
            [lanes_of(s, kind) for s, kind in pairs], None, pairs,
        )
        for kind in range(2):
            at = (step, slice(0, 1), slice(kind * LANES, (kind + 1) * LANES))
            columns[at] = jnp.maximum(
                columns[at], turned(best[kind * LANES:(kind + 1) * LANES, :])
            )

    def advance(step, _):
        far_copy(step).wait_recv()
        pl.when(core == 0)(lambda: extra_far(step).start())

        @pl.when(x == 0)
        def _():
            for part in range(PIECES):
                hop_copy(step, part).wait_recv()
                pass_copy(step, part).start()

        near_copy(step).wait_recv()
        swap_copy(step).start()
        for known in range(1, STEPS):
            pl.when(step == known)(functools.partial(older, known))
        extra_own(step).wait_recv()
        swap_copy(step).wait_recv()
        scores = dot(own[...], gathered[step])
        row_own[...] = fold(
            scores, id_own[...], [lanes_of(step, kind) for kind in range(4)], row_own[...],
            [(step, kind) for kind in range(4)],
        )
        for known in range(STEPS):
            pl.when(step == known)(functools.partial(newer, known))
        return 0

    lax.fori_loop(0, STEPS, advance, 0)

    best = jnp.max(columns[...], axis=1)
    for kind in range(4):
        reply[kind] = best[:, kind * LANES:(kind + 1) * LANES]

    def answer(kind, target):
        return remote(
            reply.at[kind], heard.at[kind], reply_s.at[kind], reply_r.at[kind], target
        )

    answer(2, device(3, core)).start()
    answer(0, device(1, core)).start()
    answer(1, device(1, 1 - core)).start()
    pl.when(core == 0)(lambda: answer(3, partner).start())
    pl.when(core == 1)(lambda: answer(3, device(3, 0)).start())
    best = jnp.concatenate([turned(row_own[chunk_rows(g), :]) for g in range(STEPS)], axis=0)
    for kind in range(4):
        answer(kind, partner).wait_recv()
        best = jnp.maximum(best, heard[kind])
    out[...] = best

    def drain(step, _):
        near_copy(step).wait_send()
        far_copy(step).wait_send()
        swap_copy(step).wait_send()
        extra_own(step).wait_send()

        @pl.when(x == 0)
        def _():
            remote(
                chunk(step), slot(step, 0), hop_s.at[step], near_r.at[step], partner
            ).wait_send()

        return 0

    lax.fori_loop(0, STEPS, drain, 0)
    for kind in range(4):
        answer(kind, partner).wait_send()


def shards(embeddings, offsets):
    block = pltpu.VMEM((ROWS, WIDTH), jnp.bfloat16)
    wide = pltpu.VMEM((ROWS, LANES), jnp.float32)
    steps = pltpu.SemaphoreType.DMA((STEPS,))
    best = pl.pallas_call(
        kernel,
        out_shape=jax.ShapeDtypeStruct((STEPS, LANES), jnp.float32),
        in_specs=[
            pl.BlockSpec(memory_space=pl.ANY),
            pl.BlockSpec(memory_space=pltpu.SMEM),
        ],
        out_specs=pl.BlockSpec(memory_space=pltpu.VMEM),
        scratch_shapes=[
            block, block, block,
            pltpu.VMEM((STEPS, 4 * CHUNK, WIDTH), jnp.bfloat16),
            wide,
            pltpu.VMEM((STEPS, 3 * LANES, LANES), jnp.float32),
            pltpu.VMEM((STEPS, 1, LANES), jnp.float32),
            pltpu.VMEM((STEPS, 1, 4 * LANES), jnp.float32),
            pltpu.VMEM((2 * LANES, LANES), jnp.int32),
            wide,
            pltpu.VMEM((STEPS, 8, 4 * LANES), jnp.float32),
            pltpu.VMEM((4, STEPS, LANES), jnp.float32),
            pltpu.VMEM((4, STEPS, LANES), jnp.float32),
            steps,
            steps, steps, steps, steps, steps, pltpu.SemaphoreType.DMA((4,)),
            pltpu.SemaphoreType.DMA((STEPS, PIECES)),
            steps, steps, steps, steps, pltpu.SemaphoreType.DMA((4,)),
        ],
        compiler_params=pltpu.CompilerParams(
            collective_id=0, has_side_effects=True, vmem_limit_bytes=62 * 1024 * 1024
        ),
        name="match",
    )(embeddings, offsets)
    return best.reshape(-1)


def solution(mesh):
    return jax.shard_map(
        shards,
        mesh=mesh,
        in_specs=(P(AXES, None), P()),
        out_specs=P(AXES),
        check_vma=False,
    )
```

```python
import functools

import jax
import jax.numpy as jnp
from jax import lax
from jax.experimental import pallas as pl
from jax.experimental.pallas import tpu as pltpu
from jax.sharding import PartitionSpec as P

AXES = ("grp", "work")
MESH = pl.DeviceIdType.MESH
ROWS = 1024
WIDTH = 1024
STEPS = 8
CHUNK = ROWS // STEPS
CHIPS = 64
DEVICES = 2 * CHIPS
LANES = 128


def dot(left, right):
    return lax.dot_general(
        left, right, (((1,), (1,)), ((), ())), preferred_element_type=jnp.float32
    )


def kernel(
    emb, offs, out,
    raw, own, moved, gathered,
    id_own, id_base, id_rows, lane_own, lane_ids, table, row_own, row_base, columns, reply, heard,
    raw_sem, near_s, far_s, base_s, swap_s, extra_s, reply_s,
    near_r, far_r, base_r, swap_r, extra_r, reply_r,
):
    grp = lax.axis_index("grp")
    work = lax.axis_index("work")
    core = work % 2
    x = (work // 2) % 4
    chip = grp * 16 + work // 2
    me = chip * 2 + core

    def device(distance, which):
        target = (chip + distance + CHIPS) % CHIPS
        return (target // 16, (target % 16) * 2 + which)

    partner = device(0, 1 - core)

    last = x == 3
    to_base = jnp.where(last, -4, 0)
    to_near = to_base + 1
    to_far = to_base + 3
    near_host = device(jnp.where(x == 0, 3, -1), core)
    far_host = device(jnp.where(x == 2, 1, -3), core)
    base_host = device(4, core)

    def remote(src, dst, send, recv, target):
        return pltpu.make_async_remote_copy(
            src_ref=src, dst_ref=dst, send_sem=send, recv_sem=recv,
            device_id=target, device_id_type=MESH,
        )

    barrier = pltpu.get_barrier_semaphore()

    def greet(target):
        pl.semaphore_signal(barrier, inc=1, device_id=target, device_id_type=MESH)

    greet(device(to_far, core))
    greet(device(to_near, core))
    pl.when(last)(lambda: greet(device(-4, core)))
    greet(partner)

    def chunk_rows(step):
        return pl.ds(pl.multiple_of(step * CHUNK, CHUNK), CHUNK)

    def chunk(step):
        return own.at[chunk_rows(step)]

    def load(step):
        return pltpu.make_async_copy(
            emb.at[chunk_rows(step)], raw.at[chunk_rows(step)], raw_sem.at[step]
        )

    for step in range(STEPS):
        load(step).start()

    def normalize(step):
        load(step).wait()
        rows = chunk_rows(step)
        wide = raw[rows, :].astype(jnp.float32)
        mean = jnp.sum(wide * wide, axis=1, keepdims=True) * (1.0 / WIDTH)
        factor = lax.rsqrt(mean + 1e-06) * (1.0 / 32.0)
        own[rows, :] = (wide * factor).astype(jnp.bfloat16)

    def slot(step, kind):
        return gathered.at[step, kind * CHUNK:(kind + 1) * CHUNK]

    def near_copy(step):
        return remote(chunk(step), slot(step, 0), near_s.at[step], near_r.at[step], near_host)

    def far_copy(step):
        return remote(chunk(step), slot(step, 2), far_s.at[step], far_r.at[step], far_host)

    def base_chunk(step):
        return moved.at[chunk_rows(step)]

    def base_copy(step):
        return remote(chunk(step), base_chunk(step), base_s.at[step], base_r.at[step], base_host)

    def swap_copy(step):
        return remote(slot(step, 0), slot(step, 1), swap_s.at[step], swap_r.at[step], partner)

    def extra_own(step):
        return remote(chunk(step), slot(step, 3), extra_s.at[step], extra_r.at[step], partner)

    def extra_far(step):
        return remote(slot(step, 2), slot(step, 3), extra_s.at[step], extra_r.at[step], partner)

    def extra_base(step):
        return remote(base_chunk(step), slot(step, 3), extra_s.at[step], extra_r.at[step], partner)

    def send(step):
        far_copy(step).start()
        near_copy(step).start()
        pl.when(last)(lambda: base_copy(step).start())
        pl.when((core == 1) & (x < 3))(lambda: extra_own(step).start())

    normalize(0)
    normalize(1)

    @pl.when(last)
    def _():
        pl.semaphore_wait(barrier, 4)

    @pl.when(x < 3)
    def _():
        pl.semaphore_wait(barrier, 3)

    send(0)

    def start(step, _):
        normalize(step)
        send(step - 1)
        return 0

    lax.fori_loop(2, STEPS, start, 0)

    def fill_table(index, _):
        table[pl.ds(index, 1), :] = jnp.full((1, LANES), offs[index], jnp.int32)
        return 0

    lax.fori_loop(0, 2 * LANES, fill_table, 0, unroll=8)
    send(STEPS - 1)

    def ids_of(owner, group):
        first = (owner % DEVICES) * ROWS + group * LANES
        index = first + lax.broadcasted_iota(jnp.int32, (1, LANES), 1)
        return jnp.sum(jnp.where(table[...] <= index, 1.0, 0.0), axis=0, keepdims=True)

    base = (me + 2 * to_base + DEVICES) % DEVICES
    extra_owner = jnp.where(core == 0, base + 1, base + 5)

    def fill_ids(group, _):
        mine = ids_of(me, group)
        lane_own[group] = mine
        id_own[chunk_rows(group), :] = jnp.broadcast_to(mine, (LANES, LANES)).T
        id_base[chunk_rows(group), :] = jnp.broadcast_to(ids_of(base, group), (LANES, LANES)).T
        owners = (base + 2, base + 3 - 2 * core, base + 6, extra_owner)
        for kind in range(4):
            ids = ids_of(owners[kind], group)
            lane_ids[group, :, kind * LANES:(kind + 1) * LANES] = ids
            if kind < 3:
                id_rows[group, kind * LANES:(kind + 1) * LANES, :] = jnp.broadcast_to(
                    ids, (LANES, LANES)
                ).T
        return 0

    lax.fori_loop(0, STEPS, fill_ids, 0)
    row_own[...] = jnp.full_like(row_own, -1.0)
    row_base[...] = jnp.full_like(row_base, -1.0)
    columns[...] = jnp.full_like(columns, -1.0)

    def fold(scores, ids, lanes, carried, targets):
        for j in range(len(lanes)):
            part = scores[:, j * LANES:(j + 1) * LANES]
            part = jnp.where(ids == lanes[j], part, -1.0)
            carried = part if carried is None else jnp.maximum(carried, part)
            step, kind = targets[j]
            at = (step, slice(None), slice(kind * LANES, (kind + 1) * LANES))
            best = jnp.max(part.reshape(part.shape[0] // 8, 8, LANES), axis=0)
            columns[at] = jnp.maximum(columns[at], best)
        return carried

    def lanes_of(step, kind):
        return lane_ids[step, :, kind * LANES:(kind + 1) * LANES]

    def turned(rows):
        return jnp.max(rows.T, axis=0, keepdims=True)

    def diagonal(block, _):
        first = pl.multiple_of(block * 2 * LANES, 2 * LANES)
        scores = dot(own[...], own[pl.ds(first, 2 * LANES), :])
        rows = lax.broadcasted_iota(jnp.int32, (ROWS, LANES), 0)
        lanes = lax.broadcasted_iota(jnp.int32, (ROWS, LANES), 1) + first
        best = row_own[...]
        for j in range(2):
            part = scores[:, j * LANES:(j + 1) * LANES]
            same = (id_own[...] == lane_own[block * 2 + j]) & (rows != lanes + j * LANES)
            best = jnp.maximum(best, jnp.where(same, part, -1.0))
        row_own[...] = best
        return 0

    lax.fori_loop(0, ROWS // (2 * LANES), diagonal, 0)

    def older(step):
        right = gathered[0:step, 0:2 * CHUNK, :].reshape(step * 2 * CHUNK, WIDTH)
        scores = dot(gathered[step, 2 * CHUNK:3 * CHUNK, :], right)
        pairs = [(s, kind) for s in range(step) for kind in range(2)]
        best = fold(
            scores, id_rows[step, 2 * CHUNK:3 * CHUNK, :],
            [lanes_of(s, kind) for s, kind in pairs], None, pairs,
        )
        at = (step, slice(0, 1), slice(2 * LANES, 3 * LANES))
        columns[at] = jnp.maximum(columns[at], turned(best))

    def newer(step):
        right = gathered[0:step + 1, 2 * CHUNK:3 * CHUNK, :].reshape((step + 1) * CHUNK, WIDTH)
        scores = dot(gathered[step, 0:2 * CHUNK, :], right)
        pairs = [(s, 2) for s in range(step + 1)]
        best = fold(
            scores, id_rows[step, 0:2 * CHUNK, :],
            [lanes_of(s, kind) for s, kind in pairs], None, pairs,
        )
        for kind in range(2):
            at = (step, slice(0, 1), slice(kind * LANES, (kind + 1) * LANES))
            columns[at] = jnp.maximum(
                columns[at], turned(best[kind * LANES:(kind + 1) * LANES, :])
            )

    kinds = range(4)

    def base_older(step):
        pairs = [(s, kind) for s in range(step) for kind in kinds]
        rows = slice(step * CHUNK, (step + 1) * CHUNK)
        scores = dot(moved[rows, :], gathered[0:step].reshape(step * 4 * CHUNK, WIDTH))
        row_base[rows, :] = fold(
            scores, id_base[rows, :], [lanes_of(s, kind) for s, kind in pairs],
            row_base[rows, :], pairs,
        )

    def base_newer(step):
        rows = slice(0, (step + 1) * CHUNK)
        scores = dot(moved[rows, :], gathered[step])
        row_base[rows, :] = fold(
            scores, id_base[rows, :], [lanes_of(step, kind) for kind in kinds],
            row_base[rows, :], [(step, kind) for kind in kinds],
        )

    def advance(step, _):
        far_copy(step).wait_recv()
        pl.when(core == 0)(lambda: extra_far(step).start())

        @pl.when(last)
        def _():
            base_copy(step).wait_recv()
            pl.when(core == 1)(lambda: extra_base(step).start())

        near_copy(step).wait_recv()
        swap_copy(step).start()
        for known in range(1, STEPS):
            pl.when(step == known)(functools.partial(older, known))
            pl.when((step == known) & last)(functools.partial(base_older, known))
        extra_own(step).wait_recv()
        swap_copy(step).wait_recv()

        @pl.when(x < 3)
        def _():
            scores = dot(own[...], gathered[step])
            row_base[...] = fold(
                scores, id_base[...], [lanes_of(step, kind) for kind in kinds], row_base[...],
                [(step, kind) for kind in kinds],
            )

        for known in range(STEPS):
            pl.when((step == known) & last)(functools.partial(base_newer, known))
            pl.when(step == known)(functools.partial(newer, known))
        return 0

    lax.fori_loop(0, STEPS, advance, 0)

    best = jnp.max(columns[...], axis=1)
    for kind in range(4):
        reply[kind] = best[:, kind * LANES:(kind + 1) * LANES]

    def answer(kind, target):
        return remote(
            reply.at[kind], heard.at[kind], reply_s.at[kind], reply_r.at[kind], target
        )

    def flat(ref):
        return jnp.concatenate([turned(ref[chunk_rows(g), :]) for g in range(STEPS)], axis=0)

    answer(2, device(to_far, core)).start()
    answer(0, device(to_near, core)).start()
    answer(1, device(to_near, 1 - core)).start()
    pl.when(core == 0)(lambda: answer(3, device(to_base, 1)).start())
    pl.when(core == 1)(lambda: answer(3, device(to_far, 0)).start())
    based = flat(row_base)
    reply[4] = based
    best = flat(row_own)

    @pl.when(last)
    def _():
        answer(4, device(-4, core)).start()
        answer(4, device(-4, core)).wait_recv()

    @pl.when(x < 3)
    def _():
        heard[4] = based

    for kind in range(4):
        answer(kind, partner).wait_recv()
        best = jnp.maximum(best, heard[kind])
    out[...] = jnp.maximum(best, heard[4])

    def drain(step, _):
        near_copy(step).wait_send()
        far_copy(step).wait_send()
        swap_copy(step).wait_send()
        extra_own(step).wait_send()

        pl.when(last)(lambda: base_copy(step).wait_send())
        return 0

    lax.fori_loop(0, STEPS, drain, 0)
    for kind in range(4):
        answer(kind, partner).wait_send()
    pl.when(last)(lambda: answer(4, partner).wait_send())


def shards(embeddings, offsets):
    block = pltpu.VMEM((ROWS, WIDTH), jnp.bfloat16)
    wide = pltpu.VMEM((ROWS, LANES), jnp.float32)
    steps = pltpu.SemaphoreType.DMA((STEPS,))
    best = pl.pallas_call(
        kernel,
        out_shape=jax.ShapeDtypeStruct((STEPS, LANES), jnp.float32),
        in_specs=[
            pl.BlockSpec(memory_space=pl.ANY),
            pl.BlockSpec(memory_space=pltpu.SMEM),
        ],
        out_specs=pl.BlockSpec(memory_space=pltpu.VMEM),
        scratch_shapes=[
            block, block, block,
            pltpu.VMEM((STEPS, 4 * CHUNK, WIDTH), jnp.bfloat16),
            wide, wide,
            pltpu.VMEM((STEPS, 3 * LANES, LANES), jnp.float32),
            pltpu.VMEM((STEPS, 1, LANES), jnp.float32),
            pltpu.VMEM((STEPS, 1, 4 * LANES), jnp.float32),
            pltpu.VMEM((2 * LANES, LANES), jnp.int32),
            wide, wide,
            pltpu.VMEM((STEPS, 8, 4 * LANES), jnp.float32),
            pltpu.VMEM((5, STEPS, LANES), jnp.float32),
            pltpu.VMEM((5, STEPS, LANES), jnp.float32),
            steps,
            steps, steps, steps, steps, steps, pltpu.SemaphoreType.DMA((5,)),
            steps, steps, steps, steps, steps, pltpu.SemaphoreType.DMA((5,)),
        ],
        compiler_params=pltpu.CompilerParams(
            collective_id=0, has_side_effects=True, vmem_limit_bytes=62 * 1024 * 1024
        ),
        name="match",
    )(embeddings, offsets)
    return best.reshape(-1)


def solution(mesh):
    return jax.shard_map(
        shards,
        mesh=mesh,
        in_specs=(P(AXES, None), P()),
        out_specs=P(AXES),
        check_vma=False,
    )
```

```python
import functools

import jax
import jax.numpy as jnp
from jax import lax
from jax.experimental import pallas as pl
from jax.experimental.pallas import tpu as pltpu
from jax.sharding import PartitionSpec as P

AXES = ("grp", "work")
MESH = pl.DeviceIdType.MESH
ROWS = 1024
WIDTH = 1024
STEPS = 8
CHUNK = ROWS // STEPS
CHIPS = 64
BASE, FAR, NEAR, SWAP, EXTRA = range(5)
DEVICES = 2 * CHIPS
LANES = 128


def dot(left, right):
    return lax.dot_general(
        left, right, (((1,), (1,)), ((), ())), preferred_element_type=jnp.float32
    )


def kernel(
    emb, offs, out,
    raw, own, mate, gathered,
    id_own, id_rows, lane_own, lane_ids, table, row_own, row_base, columns, reply, heard, mate_best,
    raw_sem, near_s, far_s, base_s, swap_s, extra_s, reply_s,
    near_r, far_r, base_r, swap_r, extra_r, reply_r, mate_sems,
):
    grp = lax.axis_index("grp")
    work = lax.axis_index("work")
    core = work % 2
    x = (work // 2) % 4
    chip = grp * 16 + work // 2
    me = chip * 2 + core

    def device(distance, which):
        target = (chip + distance + CHIPS) % CHIPS
        return (target // 16, (target % 16) * 2 + which)

    partner = device(0, 1 - core)

    last = x == 3
    to_base = jnp.where(last, -4, 0)
    to_near = to_base + 1
    to_far = to_base + 3
    near_host = device(jnp.where(x == 0, 3, -1), core)
    far_host = device(jnp.where(x == 2, 1, -3), core)
    base_host = device(4, core)
    sends_far = chip >= 2
    sends_base = last & (chip != CHIPS - 1)
    has_far = (chip != CHIPS - 3) & (chip != CHIPS - 2)
    has_base = last & (chip != 3)
    has_extra = jnp.where(core == 1, has_far, chip != 3)
    sends_extra = jnp.where(core == 0, has_far, chip != 3)
    sends_back = has_extra

    def remote(src, dst, send, recv, target):
        return pltpu.make_async_remote_copy(
            src_ref=src, dst_ref=dst, send_sem=send, recv_sem=recv,
            device_id=target, device_id_type=MESH,
        )

    barrier = pltpu.get_barrier_semaphore()

    def greet(target):
        pl.semaphore_signal(barrier, inc=1, device_id=target, device_id_type=MESH)

    pl.when(has_far)(lambda: greet(device(to_far, core)))
    greet(device(to_near, core))
    pl.when(has_base)(lambda: greet(device(-4, core)))
    greet(partner)

    def chunk_rows(step):
        return pl.ds(pl.multiple_of(step * CHUNK, CHUNK), CHUNK)

    def chunk(step):
        return own.at[chunk_rows(step)]

    def load(step):
        return pltpu.make_async_copy(
            emb.at[chunk_rows(step)], raw.at[chunk_rows(step)], raw_sem.at[step]
        )

    for step in range(STEPS):
        load(step).start()

    def normalize(step):
        load(step).wait()
        rows = chunk_rows(step)
        wide = raw[rows, :].astype(jnp.float32)
        mean = jnp.sum(wide * wide, axis=1, keepdims=True) * (1.0 / WIDTH)
        factor = lax.rsqrt(mean + 1e-06) * (1.0 / 32.0)
        own[rows, :] = (wide * factor).astype(jnp.bfloat16)

    def slot(step, kind):
        return gathered.at[step, kind * CHUNK:(kind + 1) * CHUNK]

    def near_copy(step):
        return remote(chunk(step), slot(step, NEAR), near_s.at[step], near_r.at[step], near_host)

    def far_copy(step):
        return remote(chunk(step), slot(step, FAR), far_s.at[step], far_r.at[step], far_host)

    def base_copy(step):
        return remote(chunk(step), slot(step, BASE), base_s.at[step], base_r.at[step], base_host)

    def swap_copy(step):
        return remote(slot(step, NEAR), slot(step, SWAP), swap_s.at[step], swap_r.at[step], partner)

    def extra_own(step):
        return remote(chunk(step), slot(step, EXTRA), extra_s.at[step], extra_r.at[step], partner)

    def extra_far(step):
        return remote(slot(step, FAR), slot(step, EXTRA), extra_s.at[step], extra_r.at[step], partner)

    def extra_base(step):
        return remote(slot(step, BASE), slot(step, EXTRA), extra_s.at[step], extra_r.at[step], partner)

    def send(step):
        pl.when(sends_far)(lambda: far_copy(step).start())
        near_copy(step).start()
        pl.when(sends_base)(lambda: base_copy(step).start())
        pl.when((core == 1) & (x < 3))(lambda: extra_own(step).start())

    normalize(0)
    normalize(1)

    @pl.when(sends_base)
    def _():
        pl.semaphore_wait(barrier, 4)

    @pl.when(sends_far & jnp.logical_not(sends_base))
    def _():
        pl.semaphore_wait(barrier, 3)

    @pl.when(jnp.logical_not(sends_far))
    def _():
        pl.semaphore_wait(barrier, 2)

    send(0)

    def start(step, _):
        normalize(step)
        send(step - 1)
        return 0

    lax.fori_loop(2, STEPS, start, 0)

    def fill_table(index, _):
        table[pl.ds(index, 1), :] = jnp.full((1, LANES), offs[index], jnp.int32)
        return 0

    lax.fori_loop(0, 2 * LANES, fill_table, 0, unroll=8)
    send(STEPS - 1)

    alone = chip == CHIPS - 1

    def mate_copy():
        return remote(own, mate, mate_sems.at[0], mate_sems.at[1], partner)

    def mate_answer():
        return remote(
            mate_best, heard.at[EXTRA], mate_sems.at[2], reply_r.at[EXTRA], partner
        )

    pl.when(alone & (core == 1))(lambda: mate_copy().start())

    def ids_of(owner, group):
        first = (owner % DEVICES) * ROWS + group * LANES
        index = first + lax.broadcasted_iota(jnp.int32, (1, LANES), 1)
        return jnp.sum(jnp.where(table[...] <= index, 1.0, 0.0), axis=0, keepdims=True)

    base = (me + 2 * to_base + DEVICES) % DEVICES
    extra_owner = jnp.where(core == 0, base + 1, base + 5)

    def fill_ids(group, _):
        mine = ids_of(me, group)
        lane_own[group] = mine
        id_own[chunk_rows(group), :] = jnp.broadcast_to(mine, (LANES, LANES)).T
        owners = (base, base + 6, base + 2, base + 3 - 2 * core, extra_owner)
        for kind in range(5):
            ids = ids_of(owners[kind], group)
            if kind != BASE:
                lane_ids[group, :, (kind - 1) * LANES:kind * LANES] = ids
            if kind != EXTRA:
                id_rows[group, kind * LANES:(kind + 1) * LANES, :] = jnp.broadcast_to(
                    ids, (LANES, LANES)
                ).T
        return 0

    lax.fori_loop(0, STEPS, fill_ids, 0)
    row_own[...] = jnp.full_like(row_own, -1.0)
    row_base[...] = jnp.full_like(row_base, -1.0)
    columns[...] = jnp.full_like(columns, -1.0)

    def fill(kind):
        def one(step, _):
            gathered[step, kind * CHUNK:(kind + 1) * CHUNK, :] = own[chunk_rows(step), :]
            return 0
        lax.fori_loop(0, STEPS, one, 0)

    pl.when(jnp.logical_not(has_far))(lambda: fill(FAR))
    pl.when(last & jnp.logical_not(has_base))(lambda: fill(BASE))
    pl.when(jnp.logical_not(has_extra))(lambda: fill(EXTRA))

    def place(step, kind, rows=slice(None)):
        return (step, rows, slice((kind - 1) * LANES, kind * LANES))

    def raise_to(target, part):
        best = jnp.max(part.reshape(part.shape[0] // 8, 8, LANES), axis=0)
        columns[place(*target)] = jnp.maximum(columns[place(*target)], best)

    def fold(scores, ids, lanes, carried, targets):
        for j in range(len(lanes)):
            part = scores[:, j * LANES:(j + 1) * LANES]
            part = jnp.where(ids == lanes[j], part, -1.0)
            carried = part if carried is None else jnp.maximum(carried, part)
            raise_to(targets[j], part)
        return carried

    def lanes_of(step, kind):
        return lane_ids[step, :, (kind - 1) * LANES:kind * LANES]

    def turned(rows):
        return jnp.max(rows.T, axis=0, keepdims=True)

    def diagonal(block, _):
        first = pl.multiple_of(block * 2 * LANES, 2 * LANES)
        scores = dot(own[...], own[pl.ds(first, 2 * LANES), :])
        rows = lax.broadcasted_iota(jnp.int32, (ROWS, LANES), 0)
        lanes = lax.broadcasted_iota(jnp.int32, (ROWS, LANES), 1) + first
        best = row_own[...]
        for j in range(2):
            part = scores[:, j * LANES:(j + 1) * LANES]
            same = (id_own[...] == lane_own[block * 2 + j]) & (rows != lanes + j * LANES)
            best = jnp.maximum(best, jnp.where(same, part, -1.0))
        row_own[...] = best
        return 0

    lax.fori_loop(0, ROWS // (2 * LANES), diagonal, 0)

    @pl.when(alone & (core == 0))
    def _():
        mate_copy().wait_recv()

        def against(block, _):
            first = pl.multiple_of(block * 2 * LANES, 2 * LANES)
            scores = dot(own[...], mate[pl.ds(first, 2 * LANES), :])
            best = row_own[...]
            for j in range(2):
                same = id_own[...] == ids_of(me + 1, block * 2 + j)
                part = jnp.where(same, scores[:, j * LANES:(j + 1) * LANES], -1.0)
                best = jnp.maximum(best, part)
                mate_best[pl.ds(block * 2 + j, 1), :] = jnp.max(part, axis=0, keepdims=True)
            row_own[...] = best
            return 0

        lax.fori_loop(0, ROWS // (2 * LANES), against, 0)
        mate_answer().start()

    def settle(step, kind, rows):
        at = place(step, kind, slice(0, 1))
        columns[at] = jnp.maximum(columns[at], turned(rows))

    def older(step):
        right = gathered[0:step, NEAR * CHUNK:EXTRA * CHUNK, :].reshape(step * 2 * CHUNK, WIDTH)
        scores = dot(gathered[step, FAR * CHUNK:NEAR * CHUNK, :], right)
        pairs = [(s, kind) for s in range(step) for kind in (NEAR, SWAP)]
        best = fold(
            scores, id_rows[step, FAR * CHUNK:NEAR * CHUNK, :],
            [lanes_of(s, kind) for s, kind in pairs], None, pairs,
        )
        settle(step, FAR, best)

    def older_both(step):
        right = gathered[0:step, FAR * CHUNK:, :].reshape(step * 4 * CHUNK, WIDTH)
        scores = dot(gathered[step, 0:NEAR * CHUNK, :], right)
        base_ids = id_rows[step, 0:CHUNK, :]
        far_ids = id_rows[step, CHUNK:2 * CHUNK, :]
        rows = slice(step * CHUNK, (step + 1) * CHUNK)
        best_base, best_far = row_base[rows, :], jnp.full((CHUNK, LANES), -1.0, jnp.float32)
        for j, (s, kind) in enumerate((s, kind) for s in range(step) for kind in range(1, 5)):
            lanes = lanes_of(s, kind)
            part = jnp.where(base_ids == lanes, scores[0:CHUNK, j * LANES:(j + 1) * LANES], -1.0)
            best_base = jnp.maximum(best_base, part)
            if kind in (NEAR, SWAP):
                more = jnp.where(
                    far_ids == lanes, scores[CHUNK:, j * LANES:(j + 1) * LANES], -1.0
                )
                best_far = jnp.maximum(best_far, more)
                part = jnp.maximum(part, more)
            raise_to((s, kind), part)
        row_base[rows, :] = best_base
        settle(step, FAR, best_far)

    def newer(step):
        right = gathered[0:step + 1, FAR * CHUNK:NEAR * CHUNK, :].reshape((step + 1) * CHUNK, WIDTH)
        scores = dot(gathered[step, NEAR * CHUNK:EXTRA * CHUNK, :], right)
        pairs = [(s, FAR) for s in range(step + 1)]
        best = fold(
            scores, id_rows[step, NEAR * CHUNK:EXTRA * CHUNK, :],
            [lanes_of(s, kind) for s, kind in pairs], None, pairs,
        )
        settle(step, NEAR, best[0:CHUNK, :])
        settle(step, SWAP, best[CHUNK:, :])

    kinds = range(1, 5)

    def base_newer(step):
        count = (step + 1) * CHUNK
        left = gathered[0:step + 1, 0:CHUNK, :].reshape(count, WIDTH)
        ids = id_rows[0:step + 1, 0:CHUNK, :].reshape(count, LANES)
        row_base[0:count, :] = fold(
            dot(left, gathered[step, FAR * CHUNK:, :]), ids,
            [lanes_of(step, kind) for kind in kinds], row_base[0:count, :],
            [(step, kind) for kind in kinds],
        )

    def advance(step, _):
        @pl.when(has_far)
        def _():
            far_copy(step).wait_recv()
            pl.when(core == 0)(lambda: extra_far(step).start())

        @pl.when(has_base)
        def _():
            base_copy(step).wait_recv()
            pl.when(core == 1)(lambda: extra_base(step).start())

        near_copy(step).wait_recv()
        swap_copy(step).start()
        for known in range(1, STEPS):
            pl.when((step == known) & (x < 3))(functools.partial(older, known))
            pl.when((step == known) & last)(functools.partial(older_both, known))
        pl.when(has_extra)(lambda: extra_own(step).wait_recv())
        swap_copy(step).wait_recv()

        @pl.when(x < 3)
        def _():
            scores = dot(own[...], gathered[step, FAR * CHUNK:, :])
            row_base[...] = fold(
                scores, id_own[...], [lanes_of(step, kind) for kind in kinds], row_base[...],
                [(step, kind) for kind in kinds],
            )

        for known in range(STEPS):
            pl.when((step == known) & last)(functools.partial(base_newer, known))
            pl.when(step == known)(functools.partial(newer, known))
        return 0

    lax.fori_loop(0, STEPS, advance, 0)

    best = jnp.max(columns[...], axis=1)
    for kind in kinds:
        reply[kind] = best[:, (kind - 1) * LANES:kind * LANES]

    def answer(kind, target):
        return remote(
            reply.at[kind], heard.at[kind], reply_s.at[kind], reply_r.at[kind], target
        )

    def flat(ref):
        return jnp.concatenate([turned(ref[chunk_rows(g), :]) for g in range(STEPS)], axis=0)

    pl.when(has_far)(lambda: answer(FAR, device(to_far, core)).start())
    answer(NEAR, device(to_near, core)).start()
    answer(SWAP, device(to_near, 1 - core)).start()
    pl.when((core == 0) & sends_back)(lambda: answer(EXTRA, device(to_base, 1)).start())
    pl.when((core == 1) & sends_back)(lambda: answer(EXTRA, device(to_far, 0)).start())
    based = flat(row_base)
    reply[BASE] = based
    best = flat(row_own)
    pl.when(has_base)(lambda: answer(BASE, device(-4, core)).start())
    nothing = jnp.full((STEPS, LANES), -1.0, jnp.float32)

    def hear(kind, comes, instead):
        @pl.when(comes)
        def _():
            answer(kind, partner).wait_recv()

        @pl.when(jnp.logical_not(comes))
        def _():
            heard[kind] = instead

    hear(BASE, sends_base, jnp.where(last, nothing, based))
    hear(FAR, sends_far, nothing)
    hear(EXTRA, (core == 1) | sends_far, nothing)
    answer(NEAR, partner).wait_recv()
    answer(SWAP, partner).wait_recv()
    for kind in range(5):
        best = jnp.maximum(best, heard[kind])
    out[...] = best

    def drain(step, _):
        near_copy(step).wait_send()
        pl.when(sends_far)(lambda: far_copy(step).wait_send())
        swap_copy(step).wait_send()
        pl.when(sends_extra)(lambda: extra_own(step).wait_send())

        pl.when(sends_base)(lambda: base_copy(step).wait_send())
        return 0

    lax.fori_loop(0, STEPS, drain, 0)
    answer(NEAR, partner).wait_send()
    answer(SWAP, partner).wait_send()
    pl.when(has_far)(lambda: answer(FAR, partner).wait_send())
    pl.when(has_base)(lambda: answer(BASE, partner).wait_send())
    pl.when(sends_back)(lambda: answer(EXTRA, partner).wait_send())
    pl.when(alone & (core == 1))(lambda: mate_copy().wait_send())
    pl.when(alone & (core == 0))(lambda: mate_answer().wait_send())


def shards(embeddings, offsets):
    block = pltpu.VMEM((ROWS, WIDTH), jnp.bfloat16)
    wide = pltpu.VMEM((ROWS, LANES), jnp.float32)
    steps = pltpu.SemaphoreType.DMA((STEPS,))
    best = pl.pallas_call(
        kernel,
        out_shape=jax.ShapeDtypeStruct((STEPS, LANES), jnp.float32),
        in_specs=[
            pl.BlockSpec(memory_space=pl.ANY),
            pl.BlockSpec(memory_space=pltpu.SMEM),
        ],
        out_specs=pl.BlockSpec(memory_space=pltpu.VMEM),
        scratch_shapes=[
            block, block, block,
            pltpu.VMEM((STEPS, 5 * CHUNK, WIDTH), jnp.bfloat16),
            wide,
            pltpu.VMEM((STEPS, 4 * LANES, LANES), jnp.float32),
            pltpu.VMEM((STEPS, 1, LANES), jnp.float32),
            pltpu.VMEM((STEPS, 1, 4 * LANES), jnp.float32),
            pltpu.VMEM((2 * LANES, LANES), jnp.int32),
            wide, wide,
            pltpu.VMEM((STEPS, 8, 4 * LANES), jnp.float32),
            pltpu.VMEM((5, STEPS, LANES), jnp.float32),
            pltpu.VMEM((5, STEPS, LANES), jnp.float32),
            pltpu.VMEM((STEPS, LANES), jnp.float32),
            steps,
            steps, steps, steps, steps, steps, pltpu.SemaphoreType.DMA((5,)),
            steps, steps, steps, steps, steps, pltpu.SemaphoreType.DMA((5,)),
            pltpu.SemaphoreType.DMA((3,)),
        ],
        compiler_params=pltpu.CompilerParams(
            collective_id=0, has_side_effects=True, vmem_limit_bytes=62 * 1024 * 1024
        ),
        name="match",
    )(embeddings, offsets)
    return best.reshape(-1)


def solution(mesh):
    return jax.shard_map(
        shards,
        mesh=mesh,
        in_specs=(P(AXES, None), P()),
        out_specs=P(AXES),
        check_vma=False,
    )
```

```python
import functools

import jax
import jax.numpy as jnp
from jax import lax
from jax.experimental import pallas as pl
from jax.experimental.pallas import tpu as pltpu
from jax.sharding import PartitionSpec as P

AXES = ("grp", "work")
MESH = pl.DeviceIdType.MESH
ROWS = 1024
WIDTH = 1024
STEPS = 8
CHUNK = ROWS // STEPS
CHIPS = 64
BASE, FAR, NEAR, SWAP, EXTRA = range(5)
DEVICES = 2 * CHIPS
LANES = 128


def dot(left, right):
    return lax.dot_general(
        left, right, (((1,), (1,)), ((), ())), preferred_element_type=jnp.float32
    )


def kernel(
    emb, offs, out,
    raw, own, mate, gathered,
    id_own, id_rows, lane_own, lane_ids, table, row_own, row_base, columns, reply, heard, mate_best,
    raw_sem, near_s, far_s, base_s, swap_s, extra_s, reply_s,
    near_r, far_r, base_r, swap_r, extra_r, reply_r, mate_sems,
):
    grp = lax.axis_index("grp")
    work = lax.axis_index("work")
    core = work % 2
    x = (work // 2) % 4
    chip = grp * 16 + work // 2
    me = chip * 2 + core

    def device(distance, which):
        target = (chip + distance + CHIPS) % CHIPS
        return (target // 16, (target % 16) * 2 + which)

    partner = device(0, 1 - core)

    last = x == 3
    to_base = jnp.where(last, -4, 0)
    to_near = to_base + 1
    to_far = to_base + 3
    near_host = device(jnp.where(x == 0, 3, -1), core)
    far_host = device(jnp.where(x == 2, 1, -3), core)
    base_host = device(4, core)
    sends_far = chip >= 2
    sends_base = last & (chip != CHIPS - 1)
    has_far = (chip != CHIPS - 3) & (chip != CHIPS - 2)
    has_base = last & (chip != 3)
    has_extra = jnp.where(core == 1, has_far, chip != 3)
    sends_extra = jnp.where(core == 0, has_far, chip != 3)
    sends_back = has_extra

    def remote(src, dst, send, recv, target):
        return pltpu.make_async_remote_copy(
            src_ref=src, dst_ref=dst, send_sem=send, recv_sem=recv,
            device_id=target, device_id_type=MESH,
        )

    barrier = pltpu.get_barrier_semaphore()

    def greet(target):
        pl.semaphore_signal(barrier, inc=1, device_id=target, device_id_type=MESH)

    pl.when(has_far)(lambda: greet(device(to_far, core)))
    greet(device(to_near, core))
    pl.when(has_base)(lambda: greet(device(-4, core)))
    greet(partner)

    def chunk_rows(step):
        return pl.ds(pl.multiple_of(step * CHUNK, CHUNK), CHUNK)

    def chunk(step):
        return own.at[chunk_rows(step)]

    def load(step):
        return pltpu.make_async_copy(
            emb.at[chunk_rows(step)], raw.at[chunk_rows(step)], raw_sem.at[step]
        )

    for step in range(STEPS):
        load(step).start()

    def normalize(step):
        load(step).wait()
        rows = chunk_rows(step)
        wide = raw[rows, :].astype(jnp.float32)
        mean = jnp.sum(wide * wide, axis=1, keepdims=True) * (1.0 / WIDTH)
        factor = lax.rsqrt(mean + 1e-06) * (1.0 / 32.0)
        own[rows, :] = (wide * factor).astype(jnp.bfloat16)

    def slot(step, kind):
        return gathered.at[step, kind * CHUNK:(kind + 1) * CHUNK]

    def near_copy(step):
        return remote(chunk(step), slot(step, NEAR), near_s.at[step], near_r.at[step], near_host)

    def far_copy(step):
        return remote(chunk(step), slot(step, FAR), far_s.at[step], far_r.at[step], far_host)

    def base_copy(step):
        return remote(chunk(step), slot(step, BASE), base_s.at[step], base_r.at[step], base_host)

    def swap_copy(step):
        return remote(slot(step, NEAR), slot(step, SWAP), swap_s.at[step], swap_r.at[step], partner)

    def extra_own(step):
        return remote(chunk(step), slot(step, EXTRA), extra_s.at[step], extra_r.at[step], partner)

    def extra_far(step):
        return remote(slot(step, FAR), slot(step, EXTRA), extra_s.at[step], extra_r.at[step], partner)

    def extra_base(step):
        return remote(slot(step, BASE), slot(step, EXTRA), extra_s.at[step], extra_r.at[step], partner)

    def send(step):
        pl.when(sends_far)(lambda: far_copy(step).start())
        near_copy(step).start()
        pl.when(sends_base)(lambda: base_copy(step).start())
        pl.when((core == 1) & (x < 3))(lambda: extra_own(step).start())

    normalize(0)
    normalize(1)

    @pl.when(sends_base)
    def _():
        pl.semaphore_wait(barrier, 4)

    @pl.when(sends_far & jnp.logical_not(sends_base))
    def _():
        pl.semaphore_wait(barrier, 3)

    @pl.when(jnp.logical_not(sends_far))
    def _():
        pl.semaphore_wait(barrier, 2)

    send(0)

    def start(step, _):
        normalize(step)
        send(step - 1)
        return 0

    lax.fori_loop(2, STEPS, start, 0)

    def fill_table(index, _):
        table[pl.ds(index, 1), :] = jnp.full((1, LANES), offs[index], jnp.int32)
        return 0

    lax.fori_loop(0, 2 * LANES, fill_table, 0, unroll=8)
    send(STEPS - 1)

    alone = chip == CHIPS - 1

    def mate_copy():
        return remote(own, mate, mate_sems.at[0], mate_sems.at[1], partner)

    def mate_answer():
        return remote(
            mate_best, heard.at[EXTRA], mate_sems.at[2], reply_r.at[EXTRA], partner
        )

    pl.when(alone & (core == 1))(lambda: mate_copy().start())

    def ids_of(owner, group):
        first = (owner % DEVICES) * ROWS + group * LANES
        index = first + lax.broadcasted_iota(jnp.int32, (1, LANES), 1)
        return jnp.sum(jnp.where(table[...] <= index, 1.0, 0.0), axis=0, keepdims=True)

    base = (me + 2 * to_base + DEVICES) % DEVICES
    extra_owner = jnp.where(core == 0, base + 1, base + 5)

    def fill_ids(group, _):
        mine = ids_of(me, group)
        lane_own[group] = mine
        id_own[chunk_rows(group), :] = jnp.broadcast_to(mine, (LANES, LANES)).T
        owners = (base, base + 6, base + 2, base + 3 - 2 * core, extra_owner)
        for kind in range(5):
            ids = ids_of(owners[kind], group)
            if kind != BASE:
                lane_ids[group, :, (kind - 1) * LANES:kind * LANES] = ids
            if kind != EXTRA:
                id_rows[group, kind * LANES:(kind + 1) * LANES, :] = jnp.broadcast_to(
                    ids, (LANES, LANES)
                ).T
        return 0

    lax.fori_loop(0, STEPS, fill_ids, 0)
    row_own[...] = jnp.full_like(row_own, -1.0)
    row_base[...] = jnp.full_like(row_base, -1.0)
    columns[...] = jnp.full_like(columns, -1.0)

    def fill(kind):
        def one(step, _):
            gathered[step, kind * CHUNK:(kind + 1) * CHUNK, :] = own[chunk_rows(step), :]
            return 0
        lax.fori_loop(0, STEPS, one, 0)

    pl.when(jnp.logical_not(has_far))(lambda: fill(FAR))
    pl.when(last & jnp.logical_not(has_base))(lambda: fill(BASE))
    pl.when(jnp.logical_not(has_extra))(lambda: fill(EXTRA))

    def place(step, kind, rows=slice(None)):
        return (step, rows, slice((kind - 1) * LANES, kind * LANES))

    def raise_to(target, part):
        best = jnp.max(part.reshape(part.shape[0] // 8, 8, LANES), axis=0)
        columns[place(*target)] = jnp.maximum(columns[place(*target)], best)

    def fold(scores, ids, lanes, carried, targets):
        for j in range(len(lanes)):
            part = scores[:, j * LANES:(j + 1) * LANES]
            part = jnp.where(ids == lanes[j], part, -1.0)
            carried = part if carried is None else jnp.maximum(carried, part)
            raise_to(targets[j], part)
        return carried

    def lanes_of(step, kind):
        return lane_ids[step, :, (kind - 1) * LANES:kind * LANES]

    def turned(rows):
        return jnp.max(rows.T, axis=0, keepdims=True)

    def diagonal(block, _):
        first = pl.multiple_of(block * 2 * LANES, 2 * LANES)
        scores = dot(own[...], own[pl.ds(first, 2 * LANES), :])
        rows = lax.broadcasted_iota(jnp.int32, (ROWS, LANES), 0)
        lanes = lax.broadcasted_iota(jnp.int32, (ROWS, LANES), 1) + first
        best = row_own[...]
        for j in range(2):
            part = scores[:, j * LANES:(j + 1) * LANES]
            same = (id_own[...] == lane_own[block * 2 + j]) & (rows != lanes + j * LANES)
            best = jnp.maximum(best, jnp.where(same, part, -1.0))
        row_own[...] = best
        return 0

    lax.fori_loop(0, ROWS // (2 * LANES), diagonal, 0)

    @pl.when(alone & (core == 0))
    def _():
        mate_copy().wait_recv()

        def against(block, _):
            first = pl.multiple_of(block * 2 * LANES, 2 * LANES)
            scores = dot(own[...], mate[pl.ds(first, 2 * LANES), :])
            best = row_own[...]
            for j in range(2):
                same = id_own[...] == ids_of(me + 1, block * 2 + j)
                part = jnp.where(same, scores[:, j * LANES:(j + 1) * LANES], -1.0)
                best = jnp.maximum(best, part)
                mate_best[pl.ds(block * 2 + j, 1), :] = jnp.max(part, axis=0, keepdims=True)
            row_own[...] = best
            return 0

        lax.fori_loop(0, ROWS // (2 * LANES), against, 0)
        mate_answer().start()

    def settle(step, kind, rows):
        at = place(step, kind, slice(0, 1))
        columns[at] = jnp.maximum(columns[at], turned(rows))

    def older(step):
        right = gathered[0:step, NEAR * CHUNK:EXTRA * CHUNK, :].reshape(step * 2 * CHUNK, WIDTH)
        scores = dot(gathered[step, FAR * CHUNK:NEAR * CHUNK, :], right)
        pairs = [(s, kind) for s in range(step) for kind in (NEAR, SWAP)]
        best = fold(
            scores, id_rows[step, FAR * CHUNK:NEAR * CHUNK, :],
            [lanes_of(s, kind) for s, kind in pairs], None, pairs,
        )
        settle(step, FAR, best)

    def older_both(step):
        right = gathered[0:step, FAR * CHUNK:, :].reshape(step * 4 * CHUNK, WIDTH)
        scores = dot(gathered[step, 0:NEAR * CHUNK, :], right)
        base_ids = id_rows[step, 0:CHUNK, :]
        far_ids = id_rows[step, CHUNK:2 * CHUNK, :]
        rows = slice(step * CHUNK, (step + 1) * CHUNK)
        best_base, best_far = row_base[rows, :], jnp.full((CHUNK, LANES), -1.0, jnp.float32)
        for j, (s, kind) in enumerate((s, kind) for s in range(step) for kind in range(1, 5)):
            lanes = lanes_of(s, kind)
            part = jnp.where(base_ids == lanes, scores[0:CHUNK, j * LANES:(j + 1) * LANES], -1.0)
            best_base = jnp.maximum(best_base, part)
            if kind in (NEAR, SWAP):
                more = jnp.where(
                    far_ids == lanes, scores[CHUNK:, j * LANES:(j + 1) * LANES], -1.0
                )
                best_far = jnp.maximum(best_far, more)
                part = jnp.maximum(part, more)
            raise_to((s, kind), part)
        row_base[rows, :] = best_base
        settle(step, FAR, best_far)

    def newer(step):
        right = gathered[0:step + 1, FAR * CHUNK:NEAR * CHUNK, :].reshape((step + 1) * CHUNK, WIDTH)
        scores = dot(gathered[step, NEAR * CHUNK:EXTRA * CHUNK, :], right)
        pairs = [(s, FAR) for s in range(step + 1)]
        best = fold(
            scores, id_rows[step, NEAR * CHUNK:EXTRA * CHUNK, :],
            [lanes_of(s, kind) for s, kind in pairs], None, pairs,
        )
        settle(step, NEAR, best[0:CHUNK, :])
        settle(step, SWAP, best[CHUNK:, :])

    kinds = range(1, 5)

    def base_newer(step):
        count = (step + 1) * CHUNK
        left = gathered[0:step + 1, 0:CHUNK, :].reshape(count, WIDTH)
        ids = id_rows[0:step + 1, 0:CHUNK, :].reshape(count, LANES)
        row_base[0:count, :] = fold(
            dot(left, gathered[step, FAR * CHUNK:, :]), ids,
            [lanes_of(step, kind) for kind in kinds], row_base[0:count, :],
            [(step, kind) for kind in kinds],
        )

    def advance(step, _):
        @pl.when(has_far)
        def _():
            far_copy(step).wait_recv()
            pl.when(core == 0)(lambda: extra_far(step).start())

        @pl.when(has_base)
        def _():
            base_copy(step).wait_recv()
            pl.when(core == 1)(lambda: extra_base(step).start())

        near_copy(step).wait_recv()
        swap_copy(step).start()
        for known in range(1, STEPS):
            pl.when((step == known) & (x < 3))(functools.partial(older, known))
            pl.when((step == known) & last)(functools.partial(older_both, known))
        pl.when(has_extra)(lambda: extra_own(step).wait_recv())
        swap_copy(step).wait_recv()

        @pl.when(x < 3)
        def _():
            scores = dot(own[...], gathered[step, FAR * CHUNK:, :])
            row_base[...] = fold(
                scores, id_own[...], [lanes_of(step, kind) for kind in kinds], row_base[...],
                [(step, kind) for kind in kinds],
            )

        for known in range(STEPS):
            pl.when((step == known) & last)(functools.partial(base_newer, known))
            pl.when(step == known)(functools.partial(newer, known))
        return 0

    lax.fori_loop(0, STEPS, advance, 0)

    best = jnp.max(columns[...], axis=1)
    for kind in kinds:
        reply[kind] = best[:, (kind - 1) * LANES:kind * LANES]

    def answer(kind, target):
        return remote(
            reply.at[kind], heard.at[kind], reply_s.at[kind], reply_r.at[kind], target
        )

    def flat(ref):
        return jnp.concatenate([turned(ref[chunk_rows(g), :]) for g in range(STEPS)], axis=0)

    pl.when(has_far)(lambda: answer(FAR, device(to_far, core)).start())
    answer(NEAR, device(to_near, core)).start()
    answer(SWAP, device(to_near, 1 - core)).start()
    pl.when((core == 0) & sends_back)(lambda: answer(EXTRA, device(to_base, 1)).start())
    pl.when((core == 1) & sends_back)(lambda: answer(EXTRA, device(to_far, 0)).start())
    based = flat(row_base)
    reply[BASE] = based
    best = flat(row_own)
    pl.when(has_base)(lambda: answer(BASE, device(-4, core)).start())
    nothing = jnp.full((STEPS, LANES), -1.0, jnp.float32)

    def hear(kind, comes, instead):
        @pl.when(comes)
        def _():
            answer(kind, partner).wait_recv()

        @pl.when(jnp.logical_not(comes))
        def _():
            heard[kind] = instead

    hear(BASE, sends_base, jnp.where(last, nothing, based))
    hear(FAR, sends_far, nothing)
    hear(EXTRA, (core == 1) | sends_far, nothing)
    answer(NEAR, partner).wait_recv()
    answer(SWAP, partner).wait_recv()
    for kind in range(5):
        best = jnp.maximum(best, heard[kind])
    out[...] = best

    def drain(step, _):
        near_copy(step).wait_send()
        pl.when(sends_far)(lambda: far_copy(step).wait_send())
        swap_copy(step).wait_send()
        pl.when(sends_extra)(lambda: extra_own(step).wait_send())

        pl.when(sends_base)(lambda: base_copy(step).wait_send())
        return 0

    lax.fori_loop(0, STEPS, drain, 0)
    answer(NEAR, partner).wait_send()
    answer(SWAP, partner).wait_send()
    pl.when(has_far)(lambda: answer(FAR, partner).wait_send())
    pl.when(has_base)(lambda: answer(BASE, partner).wait_send())
    pl.when(sends_back)(lambda: answer(EXTRA, partner).wait_send())
    pl.when(alone & (core == 1))(lambda: mate_copy().wait_send())
    pl.when(alone & (core == 0))(lambda: mate_answer().wait_send())


def shards(embeddings, offsets):
    block = pltpu.VMEM((ROWS, WIDTH), jnp.bfloat16)
    wide = pltpu.VMEM((ROWS, LANES), jnp.float32)
    steps = pltpu.SemaphoreType.DMA((STEPS,))
    best = pl.pallas_call(
        kernel,
        out_shape=jax.ShapeDtypeStruct((STEPS, LANES), jnp.float32),
        in_specs=[
            pl.BlockSpec(memory_space=pl.ANY),
            pl.BlockSpec(memory_space=pltpu.SMEM),
        ],
        out_specs=pl.BlockSpec(memory_space=pltpu.VMEM),
        scratch_shapes=[
            block, block, block,
            pltpu.VMEM((STEPS, 5 * CHUNK, WIDTH), jnp.bfloat16),
            wide,
            pltpu.VMEM((STEPS, 4 * LANES, LANES), jnp.float32),
            pltpu.VMEM((STEPS, 1, LANES), jnp.float32),
            pltpu.VMEM((STEPS, 1, 4 * LANES), jnp.float32),
            pltpu.VMEM((2 * LANES, LANES), jnp.int32),
            wide, wide,
            pltpu.VMEM((STEPS, 8, 4 * LANES), jnp.float32),
            pltpu.VMEM((5, STEPS, LANES), jnp.float32),
            pltpu.VMEM((5, STEPS, LANES), jnp.float32),
            pltpu.VMEM((STEPS, LANES), jnp.float32),
            steps,
            steps, steps, steps, steps, steps, pltpu.SemaphoreType.DMA((5,)),
            steps, steps, steps, steps, steps, pltpu.SemaphoreType.DMA((5,)),
            pltpu.SemaphoreType.DMA((3,)),
        ],
        compiler_params=pltpu.CompilerParams(
            collective_id=0, has_side_effects=True, vmem_limit_bytes=53 * 1024 * 1024
        ),
        name="match",
    )(embeddings, offsets)
    return best.reshape(-1)


def solution(mesh):
    return jax.shard_map(
        shards,
        mesh=mesh,
        in_specs=(P(AXES, None), P()),
        out_specs=P(AXES),
        check_vma=False,
    )
```

```python
import functools

import jax
import jax.numpy as jnp
from jax import lax
from jax.experimental import pallas as pl
from jax.experimental.pallas import tpu as pltpu
from jax.sharding import PartitionSpec as P

AXES = ("grp", "work")
MESH = pl.DeviceIdType.MESH
ROWS = 1024
WIDTH = 1024
STEPS = 8
CHUNK = ROWS // STEPS
CHIPS = 64
BASE, FAR, NEAR, SWAP, EXTRA = range(5)
DEVICES = 2 * CHIPS
LANES = 128


def dot(left, right):
    return lax.dot_general(
        left, right, (((1,), (1,)), ((), ())), preferred_element_type=jnp.float32
    )


def kernel(
    emb, offs, out,
    raw, own, mate, gathered, starts,
    id_own, id_rows, lane_own, lane_ids, table, row_own, row_base, columns, reply, heard, mate_best,
    raw_sem, starts_sem, near_s, far_s, base_s, swap_s, extra_s, reply_s,
    near_r, far_r, base_r, swap_r, extra_r, reply_r, mate_sems,
):
    grp = lax.axis_index("grp")
    work = lax.axis_index("work")
    core = work % 2
    x = (work // 2) % 4
    chip = grp * 16 + work // 2
    me = chip * 2 + core

    def device(distance, which):
        target = (chip + distance + CHIPS) % CHIPS
        return (target // 16, (target % 16) * 2 + which)

    partner = device(0, 1 - core)

    last = x == 3
    to_base = jnp.where(last, -4, 0)
    to_near = to_base + 1
    to_far = to_base + 3
    near_host = device(jnp.where(x == 0, 3, -1), core)
    far_host = device(jnp.where(x == 2, 1, -3), core)
    base_host = device(4, core)
    sends_far = chip >= 2
    sends_base = last & (chip != CHIPS - 1)
    has_far = (chip != CHIPS - 3) & (chip != CHIPS - 2)
    has_base = last & (chip != 3)
    has_extra = jnp.where(core == 1, has_far, chip != 3)
    sends_extra = jnp.where(core == 0, has_far, chip != 3)
    sends_back = has_extra

    def remote(src, dst, send, recv, target):
        return pltpu.make_async_remote_copy(
            src_ref=src, dst_ref=dst, send_sem=send, recv_sem=recv,
            device_id=target, device_id_type=MESH,
        )

    barrier = pltpu.get_barrier_semaphore()

    def greet(target):
        pl.semaphore_signal(barrier, inc=1, device_id=target, device_id_type=MESH)

    pl.when(has_far)(lambda: greet(device(to_far, core)))
    greet(device(to_near, core))
    pl.when(has_base)(lambda: greet(device(-4, core)))
    greet(partner)

    def chunk_rows(step):
        return pl.ds(pl.multiple_of(step * CHUNK, CHUNK), CHUNK)

    def chunk(step):
        return own.at[chunk_rows(step)]

    def load(step):
        return pltpu.make_async_copy(
            emb.at[chunk_rows(step)], raw.at[chunk_rows(step)], raw_sem.at[step]
        )

    for step in range(STEPS):
        load(step).start()
    load_starts = pltpu.make_async_copy(offs, starts, starts_sem)
    load_starts.start()

    def normalize(step):
        load(step).wait()
        rows = chunk_rows(step)
        wide = raw[rows, :].astype(jnp.float32)
        mean = jnp.sum(wide * wide, axis=1, keepdims=True) * (1.0 / WIDTH)
        factor = lax.rsqrt(mean + 1e-06) * (1.0 / 32.0)
        own[rows, :] = (wide * factor).astype(jnp.bfloat16)

    def slot(step, kind):
        return gathered.at[step, kind * CHUNK:(kind + 1) * CHUNK]

    def near_copy(step):
        return remote(chunk(step), slot(step, NEAR), near_s.at[step], near_r.at[step], near_host)

    def far_copy(step):
        return remote(chunk(step), slot(step, FAR), far_s.at[step], far_r.at[step], far_host)

    def base_copy(step):
        return remote(chunk(step), slot(step, BASE), base_s.at[step], base_r.at[step], base_host)

    def swap_copy(step):
        return remote(slot(step, NEAR), slot(step, SWAP), swap_s.at[step], swap_r.at[step], partner)

    def extra_own(step):
        return remote(chunk(step), slot(step, EXTRA), extra_s.at[step], extra_r.at[step], partner)

    def extra_far(step):
        return remote(slot(step, FAR), slot(step, EXTRA), extra_s.at[step], extra_r.at[step], partner)

    def extra_base(step):
        return remote(slot(step, BASE), slot(step, EXTRA), extra_s.at[step], extra_r.at[step], partner)

    def send(step):
        pl.when(sends_far)(lambda: far_copy(step).start())
        near_copy(step).start()
        pl.when(sends_base)(lambda: base_copy(step).start())
        pl.when((core == 1) & (x < 3))(lambda: extra_own(step).start())

    normalize(0)
    normalize(1)

    @pl.when(sends_base)
    def _():
        pl.semaphore_wait(barrier, 4)

    @pl.when(sends_far & jnp.logical_not(sends_base))
    def _():
        pl.semaphore_wait(barrier, 3)

    @pl.when(jnp.logical_not(sends_far))
    def _():
        pl.semaphore_wait(barrier, 2)

    send(0)

    def start(step, _):
        normalize(step)
        send(step - 1)
        return 0

    lax.fori_loop(2, STEPS, start, 0)

    def fill_table(index, _):
        table[pl.ds(index, 1), :] = jnp.full((1, LANES), starts[index], jnp.int32)
        return 0

    load_starts.wait()
    lax.fori_loop(0, 2 * LANES, fill_table, 0, unroll=8)
    send(STEPS - 1)

    alone = chip == CHIPS - 1

    def mate_copy():
        return remote(own, mate, mate_sems.at[0], mate_sems.at[1], partner)

    def mate_answer():
        return remote(
            mate_best, heard.at[EXTRA], mate_sems.at[2], reply_r.at[EXTRA], partner
        )

    pl.when(alone & (core == 1))(lambda: mate_copy().start())

    def ids_of(owner, group):
        first = (owner % DEVICES) * ROWS + group * LANES
        index = first + lax.broadcasted_iota(jnp.int32, (1, LANES), 1)
        return jnp.sum(jnp.where(table[...] <= index, 1.0, 0.0), axis=0, keepdims=True)

    base = (me + 2 * to_base + DEVICES) % DEVICES
    extra_owner = jnp.where(core == 0, base + 1, base + 5)

    def fill_ids(group, _):
        mine = ids_of(me, group)
        lane_own[group] = mine
        id_own[chunk_rows(group), :] = jnp.broadcast_to(mine, (LANES, LANES)).T
        owners = (base, base + 6, base + 2, base + 3 - 2 * core, extra_owner)
        for kind in range(5):
            ids = ids_of(owners[kind], group)
            if kind != BASE:
                lane_ids[group, :, (kind - 1) * LANES:kind * LANES] = ids
            if kind != EXTRA:
                id_rows[group, kind * LANES:(kind + 1) * LANES, :] = jnp.broadcast_to(
                    ids, (LANES, LANES)
                ).T
        return 0

    lax.fori_loop(0, STEPS, fill_ids, 0)
    row_own[...] = jnp.full_like(row_own, -1.0)
    row_base[...] = jnp.full_like(row_base, -1.0)
    columns[...] = jnp.full_like(columns, -1.0)

    def fill(kind):
        def one(step, _):
            gathered[step, kind * CHUNK:(kind + 1) * CHUNK, :] = own[chunk_rows(step), :]
            return 0
        lax.fori_loop(0, STEPS, one, 0)

    pl.when(jnp.logical_not(has_far))(lambda: fill(FAR))
    pl.when(last & jnp.logical_not(has_base))(lambda: fill(BASE))
    pl.when(jnp.logical_not(has_extra))(lambda: fill(EXTRA))

    def place(step, kind, rows=slice(None)):
        return (step, rows, slice((kind - 1) * LANES, kind * LANES))

    def raise_to(target, part):
        best = jnp.max(part.reshape(part.shape[0] // 8, 8, LANES), axis=0)
        columns[place(*target)] = jnp.maximum(columns[place(*target)], best)

    def fold(scores, ids, lanes, carried, targets):
        for j in range(len(lanes)):
            part = scores[:, j * LANES:(j + 1) * LANES]
            part = jnp.where(ids == lanes[j], part, -1.0)
            carried = part if carried is None else jnp.maximum(carried, part)
            raise_to(targets[j], part)
        return carried

    def lanes_of(step, kind):
        return lane_ids[step, :, (kind - 1) * LANES:kind * LANES]

    def turned(rows):
        return jnp.max(rows.T, axis=0, keepdims=True)

    def diagonal(block, _):
        first = pl.multiple_of(block * 2 * LANES, 2 * LANES)
        scores = dot(own[...], own[pl.ds(first, 2 * LANES), :])
        rows = lax.broadcasted_iota(jnp.int32, (ROWS, LANES), 0)
        lanes = lax.broadcasted_iota(jnp.int32, (ROWS, LANES), 1) + first
        best = row_own[...]
        for j in range(2):
            part = scores[:, j * LANES:(j + 1) * LANES]
            same = (id_own[...] == lane_own[block * 2 + j]) & (rows != lanes + j * LANES)
            best = jnp.maximum(best, jnp.where(same, part, -1.0))
        row_own[...] = best
        return 0

    lax.fori_loop(0, ROWS // (2 * LANES), diagonal, 0)

    @pl.when(alone & (core == 0))
    def _():
        mate_copy().wait_recv()

        def against(block, _):
            first = pl.multiple_of(block * 2 * LANES, 2 * LANES)
            scores = dot(own[...], mate[pl.ds(first, 2 * LANES), :])
            best = row_own[...]
            for j in range(2):
                same = id_own[...] == ids_of(me + 1, block * 2 + j)
                part = jnp.where(same, scores[:, j * LANES:(j + 1) * LANES], -1.0)
                best = jnp.maximum(best, part)
                mate_best[pl.ds(block * 2 + j, 1), :] = jnp.max(part, axis=0, keepdims=True)
            row_own[...] = best
            return 0

        lax.fori_loop(0, ROWS // (2 * LANES), against, 0)
        mate_answer().start()

    def settle(step, kind, rows):
        at = place(step, kind, slice(0, 1))
        columns[at] = jnp.maximum(columns[at], turned(rows))

    def older(step):
        right = gathered[0:step, NEAR * CHUNK:EXTRA * CHUNK, :].reshape(step * 2 * CHUNK, WIDTH)
        scores = dot(gathered[step, FAR * CHUNK:NEAR * CHUNK, :], right)
        pairs = [(s, kind) for s in range(step) for kind in (NEAR, SWAP)]
        best = fold(
            scores, id_rows[step, FAR * CHUNK:NEAR * CHUNK, :],
            [lanes_of(s, kind) for s, kind in pairs], None, pairs,
        )
        settle(step, FAR, best)

    def older_both(step):
        right = gathered[0:step, FAR * CHUNK:, :].reshape(step * 4 * CHUNK, WIDTH)
        scores = dot(gathered[step, 0:NEAR * CHUNK, :], right)
        base_ids = id_rows[step, 0:CHUNK, :]
        far_ids = id_rows[step, CHUNK:2 * CHUNK, :]
        rows = slice(step * CHUNK, (step + 1) * CHUNK)
        best_base, best_far = row_base[rows, :], jnp.full((CHUNK, LANES), -1.0, jnp.float32)
        for j, (s, kind) in enumerate((s, kind) for s in range(step) for kind in range(1, 5)):
            lanes = lanes_of(s, kind)
            part = jnp.where(base_ids == lanes, scores[0:CHUNK, j * LANES:(j + 1) * LANES], -1.0)
            best_base = jnp.maximum(best_base, part)
            if kind in (NEAR, SWAP):
                more = jnp.where(
                    far_ids == lanes, scores[CHUNK:, j * LANES:(j + 1) * LANES], -1.0
                )
                best_far = jnp.maximum(best_far, more)
                part = jnp.maximum(part, more)
            raise_to((s, kind), part)
        row_base[rows, :] = best_base
        settle(step, FAR, best_far)

    def newer(step):
        right = gathered[0:step + 1, FAR * CHUNK:NEAR * CHUNK, :].reshape((step + 1) * CHUNK, WIDTH)
        scores = dot(gathered[step, NEAR * CHUNK:EXTRA * CHUNK, :], right)
        pairs = [(s, FAR) for s in range(step + 1)]
        best = fold(
            scores, id_rows[step, NEAR * CHUNK:EXTRA * CHUNK, :],
            [lanes_of(s, kind) for s, kind in pairs], None, pairs,
        )
        settle(step, NEAR, best[0:CHUNK, :])
        settle(step, SWAP, best[CHUNK:, :])

    kinds = range(1, 5)

    def base_newer(step):
        count = (step + 1) * CHUNK
        left = gathered[0:step + 1, 0:CHUNK, :].reshape(count, WIDTH)
        ids = id_rows[0:step + 1, 0:CHUNK, :].reshape(count, LANES)
        row_base[0:count, :] = fold(
            dot(left, gathered[step, FAR * CHUNK:, :]), ids,
            [lanes_of(step, kind) for kind in kinds], row_base[0:count, :],
            [(step, kind) for kind in kinds],
        )

    def advance(step, _):
        @pl.when(has_far)
        def _():
            far_copy(step).wait_recv()
            pl.when(core == 0)(lambda: extra_far(step).start())

        @pl.when(has_base)
        def _():
            base_copy(step).wait_recv()
            pl.when(core == 1)(lambda: extra_base(step).start())

        near_copy(step).wait_recv()
        swap_copy(step).start()
        for known in range(1, STEPS):
            pl.when((step == known) & (x < 3))(functools.partial(older, known))
            pl.when((step == known) & last)(functools.partial(older_both, known))
        pl.when(has_extra)(lambda: extra_own(step).wait_recv())
        swap_copy(step).wait_recv()

        @pl.when(x < 3)
        def _():
            scores = dot(own[...], gathered[step, FAR * CHUNK:, :])
            row_base[...] = fold(
                scores, id_own[...], [lanes_of(step, kind) for kind in kinds], row_base[...],
                [(step, kind) for kind in kinds],
            )

        for known in range(STEPS):
            pl.when((step == known) & last)(functools.partial(base_newer, known))
            pl.when(step == known)(functools.partial(newer, known))
        return 0

    lax.fori_loop(0, STEPS, advance, 0)

    best = jnp.max(columns[...], axis=1)
    for kind in kinds:
        reply[kind] = best[:, (kind - 1) * LANES:kind * LANES]

    def answer(kind, target):
        return remote(
            reply.at[kind], heard.at[kind], reply_s.at[kind], reply_r.at[kind], target
        )

    def flat(ref):
        return jnp.concatenate([turned(ref[chunk_rows(g), :]) for g in range(STEPS)], axis=0)

    pl.when(has_far)(lambda: answer(FAR, device(to_far, core)).start())
    answer(NEAR, device(to_near, core)).start()
    answer(SWAP, device(to_near, 1 - core)).start()
    pl.when((core == 0) & sends_back)(lambda: answer(EXTRA, device(to_base, 1)).start())
    pl.when((core == 1) & sends_back)(lambda: answer(EXTRA, device(to_far, 0)).start())
    based = flat(row_base)
    reply[BASE] = based
    best = flat(row_own)
    pl.when(has_base)(lambda: answer(BASE, device(-4, core)).start())
    nothing = jnp.full((STEPS, LANES), -1.0, jnp.float32)

    def hear(kind, comes, instead):
        @pl.when(comes)
        def _():
            answer(kind, partner).wait_recv()

        @pl.when(jnp.logical_not(comes))
        def _():
            heard[kind] = instead

    hear(BASE, sends_base, jnp.where(last, nothing, based))
    hear(FAR, sends_far, nothing)
    hear(EXTRA, (core == 1) | sends_far, nothing)
    answer(NEAR, partner).wait_recv()
    answer(SWAP, partner).wait_recv()
    for kind in range(5):
        best = jnp.maximum(best, heard[kind])
    out[...] = best

    def drain(step, _):
        near_copy(step).wait_send()
        pl.when(sends_far)(lambda: far_copy(step).wait_send())
        swap_copy(step).wait_send()
        pl.when(sends_extra)(lambda: extra_own(step).wait_send())

        pl.when(sends_base)(lambda: base_copy(step).wait_send())
        return 0

    lax.fori_loop(0, STEPS, drain, 0)
    answer(NEAR, partner).wait_send()
    answer(SWAP, partner).wait_send()
    pl.when(has_far)(lambda: answer(FAR, partner).wait_send())
    pl.when(has_base)(lambda: answer(BASE, partner).wait_send())
    pl.when(sends_back)(lambda: answer(EXTRA, partner).wait_send())
    pl.when(alone & (core == 1))(lambda: mate_copy().wait_send())
    pl.when(alone & (core == 0))(lambda: mate_answer().wait_send())


def shards(embeddings, offsets):
    block = pltpu.VMEM((ROWS, WIDTH), jnp.bfloat16)
    wide = pltpu.VMEM((ROWS, LANES), jnp.float32)
    steps = pltpu.SemaphoreType.DMA((STEPS,))
    best = pl.pallas_call(
        kernel,
        out_shape=jax.ShapeDtypeStruct((STEPS, LANES), jnp.float32),
        in_specs=[
            pl.BlockSpec(memory_space=pl.ANY),
            pl.BlockSpec(memory_space=pltpu.HBM),
        ],
        out_specs=pl.BlockSpec(memory_space=pltpu.VMEM),
        scratch_shapes=[
            block, block, block,
            pltpu.VMEM((STEPS, 5 * CHUNK, WIDTH), jnp.bfloat16),
            pltpu.SMEM((257,), jnp.int32),
            wide,
            pltpu.VMEM((STEPS, 4 * LANES, LANES), jnp.float32),
            pltpu.VMEM((STEPS, 1, LANES), jnp.float32),
            pltpu.VMEM((STEPS, 1, 4 * LANES), jnp.float32),
            pltpu.VMEM((2 * LANES, LANES), jnp.int32),
            wide, wide,
            pltpu.VMEM((STEPS, 8, 4 * LANES), jnp.float32),
            pltpu.VMEM((5, STEPS, LANES), jnp.float32),
            pltpu.VMEM((5, STEPS, LANES), jnp.float32),
            pltpu.VMEM((STEPS, LANES), jnp.float32),
            steps, pltpu.SemaphoreType.DMA(()),
            steps, steps, steps, steps, steps, pltpu.SemaphoreType.DMA((5,)),
            steps, steps, steps, steps, steps, pltpu.SemaphoreType.DMA((5,)),
            pltpu.SemaphoreType.DMA((3,)),
        ],
        compiler_params=pltpu.CompilerParams(
            collective_id=0, has_side_effects=True, vmem_limit_bytes=53 * 1024 * 1024
        ),
        name="match",
    )(embeddings, pltpu.with_memory_space_constraint(offsets, pltpu.HBM))
    return best.reshape(-1)


def solution(mesh):
    return jax.shard_map(
        shards,
        mesh=mesh,
        in_specs=(P(AXES, None), P()),
        out_specs=P(AXES),
        check_vma=False,
    )
```

```python
import functools

import jax
import jax.numpy as jnp
from jax import lax
from jax.experimental import pallas as pl
from jax.experimental.pallas import tpu as pltpu
from jax.sharding import PartitionSpec as P

AXES = ("grp", "work")
MESH = pl.DeviceIdType.MESH
ROWS = 1024
WIDTH = 1024
STEPS = 8
CHUNK = ROWS // STEPS
CHIPS = 64
BASE, FAR, NEAR, SWAP, EXTRA = range(5)
DEVICES = 2 * CHIPS
LANES = 128


def dot(left, right):
    return lax.dot_general(
        left, right, (((1,), (1,)), ((), ())), preferred_element_type=jnp.float32
    )


def kernel(
    emb, offs, out,
    raw, own, mate, gathered, starts,
    id_own, id_rows, lane_own, lane_ids, table, row_own, row_base, columns, reply, heard, mate_best,
    raw_sem, starts_sem, near_s, far_s, base_s, swap_s, extra_s, reply_s,
    near_r, far_r, base_r, swap_r, extra_r, reply_r, mate_sems,
):
    grp = lax.axis_index("grp")
    work = lax.axis_index("work")
    core = work % 2
    x = (work // 2) % 4
    chip = grp * 16 + work // 2
    me = chip * 2 + core

    def device(distance, which):
        target = (chip + distance + CHIPS) % CHIPS
        return (target // 16, (target % 16) * 2 + which)

    partner = device(0, 1 - core)

    last = x == 3
    distant = ((work // 8) == 3) & ((x == 1) | (x == 2))
    to_base = jnp.where(last, -4, 0)
    to_near = to_base + 1
    to_far = to_base + 3
    near_host = device(jnp.where(x == 0, 3, -1), core)
    far_host = device(jnp.where(x == 2, 1, -3), core)
    base_host = device(4, core)
    sends_far = chip >= 2
    sends_base = last & (chip != CHIPS - 1)
    has_far = (chip != CHIPS - 3) & (chip != CHIPS - 2)
    has_base = last & (chip != 3)
    has_extra = jnp.where(core == 1, has_far, chip != 3)
    sends_extra = jnp.where(core == 0, has_far, chip != 3)
    sends_back = has_extra

    def remote(src, dst, send, recv, target):
        return pltpu.make_async_remote_copy(
            src_ref=src, dst_ref=dst, send_sem=send, recv_sem=recv,
            device_id=target, device_id_type=MESH,
        )

    barrier = pltpu.get_barrier_semaphore()

    def greet(target):
        pl.semaphore_signal(barrier, inc=1, device_id=target, device_id_type=MESH)

    pl.when(has_far)(lambda: greet(device(to_far, core)))
    greet(device(to_near, core))
    pl.when(has_base)(lambda: greet(device(-4, core)))
    greet(partner)

    def chunk_rows(step):
        return pl.ds(pl.multiple_of(step * CHUNK, CHUNK), CHUNK)

    def chunk(step):
        return own.at[chunk_rows(step)]

    def load(step):
        return pltpu.make_async_copy(
            emb.at[chunk_rows(step)], raw.at[chunk_rows(step)], raw_sem.at[step]
        )

    for step in range(STEPS):
        load(step).start()
    load_starts = pltpu.make_async_copy(offs, starts, starts_sem)
    load_starts.start()

    def normalize(step):
        load(step).wait()
        rows = chunk_rows(step)
        wide = raw[rows, :].astype(jnp.float32)
        mean = jnp.sum(wide * wide, axis=1, keepdims=True) * (1.0 / WIDTH)
        factor = lax.rsqrt(mean + 1e-06) * (1.0 / 32.0)
        own[rows, :] = (wide * factor).astype(jnp.bfloat16)

    def slot(step, kind):
        return gathered.at[step, kind * CHUNK:(kind + 1) * CHUNK]

    def near_copy(step):
        return remote(chunk(step), slot(step, NEAR), near_s.at[step], near_r.at[step], near_host)

    def far_copy(step):
        return remote(chunk(step), slot(step, FAR), far_s.at[step], far_r.at[step], far_host)

    def base_copy(step):
        return remote(chunk(step), slot(step, BASE), base_s.at[step], base_r.at[step], base_host)

    def swap_copy(step):
        return remote(slot(step, NEAR), slot(step, SWAP), swap_s.at[step], swap_r.at[step], partner)

    def extra_own(step):
        return remote(chunk(step), slot(step, EXTRA), extra_s.at[step], extra_r.at[step], partner)

    def extra_far(step):
        return remote(slot(step, FAR), slot(step, EXTRA), extra_s.at[step], extra_r.at[step], partner)

    def extra_base(step):
        return remote(slot(step, BASE), slot(step, EXTRA), extra_s.at[step], extra_r.at[step], partner)

    def send(step):
        pl.when(sends_far)(lambda: far_copy(step).start())
        near_copy(step).start()
        pl.when(sends_base)(lambda: base_copy(step).start())
        pl.when((core == 1) & (x < 3))(lambda: extra_own(step).start())

    normalize(0)
    normalize(1)

    @pl.when(sends_base)
    def _():
        pl.semaphore_wait(barrier, 4)

    @pl.when(sends_far & jnp.logical_not(sends_base))
    def _():
        pl.semaphore_wait(barrier, 3)

    @pl.when(jnp.logical_not(sends_far))
    def _():
        pl.semaphore_wait(barrier, 2)

    send(0)

    def start(step, _):
        normalize(step)
        send(step - 1)
        return 0

    lax.fori_loop(2, STEPS, start, 0)

    def fill_table(index, _):
        table[pl.ds(index, 1), :] = jnp.full((1, LANES), starts[index], jnp.int32)
        return 0

    load_starts.wait()
    lax.fori_loop(0, 2 * LANES, fill_table, 0, unroll=8)
    send(STEPS - 1)

    alone = chip == CHIPS - 1

    def mate_copy():
        return remote(own, mate, mate_sems.at[0], mate_sems.at[1], partner)

    def mate_answer():
        return remote(
            mate_best, heard.at[EXTRA], mate_sems.at[2], reply_r.at[EXTRA], partner
        )

    pl.when(alone & (core == 1))(lambda: mate_copy().start())

    def ids_of(owner, group):
        first = (owner % DEVICES) * ROWS + group * LANES
        index = first + lax.broadcasted_iota(jnp.int32, (1, LANES), 1)
        return jnp.sum(jnp.where(table[...] <= index, 1.0, 0.0), axis=0, keepdims=True)

    base = (me + 2 * to_base + DEVICES) % DEVICES
    extra_owner = jnp.where(core == 0, base + 1, base + 5)

    def fill_ids(group, _):
        mine = ids_of(me, group)
        lane_own[group] = mine
        id_own[chunk_rows(group), :] = jnp.broadcast_to(mine, (LANES, LANES)).T
        owners = (base, base + 6, base + 2, base + 3 - 2 * core, extra_owner)
        for kind in range(5):
            ids = ids_of(owners[kind], group)
            if kind != BASE:
                lane_ids[group, :, (kind - 1) * LANES:kind * LANES] = ids
            if kind != EXTRA:
                id_rows[group, kind * LANES:(kind + 1) * LANES, :] = jnp.broadcast_to(
                    ids, (LANES, LANES)
                ).T
        return 0

    lax.fori_loop(0, STEPS, fill_ids, 0)
    row_own[...] = jnp.full_like(row_own, -1.0)
    row_base[...] = jnp.full_like(row_base, -1.0)
    columns[...] = jnp.full_like(columns, -1.0)

    def fill(kind):
        def one(step, _):
            gathered[step, kind * CHUNK:(kind + 1) * CHUNK, :] = own[chunk_rows(step), :]
            return 0
        lax.fori_loop(0, STEPS, one, 0)

    pl.when(jnp.logical_not(has_far))(lambda: fill(FAR))
    pl.when(last & jnp.logical_not(has_base))(lambda: fill(BASE))
    pl.when(jnp.logical_not(has_extra))(lambda: fill(EXTRA))

    def place(step, kind, rows=slice(None)):
        return (step, rows, slice((kind - 1) * LANES, kind * LANES))

    def raise_to(target, part):
        best = jnp.max(part.reshape(part.shape[0] // 8, 8, LANES), axis=0)
        columns[place(*target)] = jnp.maximum(columns[place(*target)], best)

    def fold(scores, ids, lanes, carried, targets):
        for j in range(len(lanes)):
            part = scores[:, j * LANES:(j + 1) * LANES]
            part = jnp.where(ids == lanes[j], part, -1.0)
            carried = part if carried is None else jnp.maximum(carried, part)
            raise_to(targets[j], part)
        return carried

    def lanes_of(step, kind):
        return lane_ids[step, :, (kind - 1) * LANES:kind * LANES]

    def turned(rows):
        return jnp.max(rows.T, axis=0, keepdims=True)

    def diagonal(block, _):
        first = pl.multiple_of(block * 2 * LANES, 2 * LANES)
        scores = dot(own[...], own[pl.ds(first, 2 * LANES), :])
        rows = lax.broadcasted_iota(jnp.int32, (ROWS, LANES), 0)
        lanes = lax.broadcasted_iota(jnp.int32, (ROWS, LANES), 1) + first
        best = row_own[...]
        for j in range(2):
            part = scores[:, j * LANES:(j + 1) * LANES]
            same = (id_own[...] == lane_own[block * 2 + j]) & (rows != lanes + j * LANES)
            best = jnp.maximum(best, jnp.where(same, part, -1.0))
        row_own[...] = best
        return 0

    lax.fori_loop(0, ROWS // (2 * LANES), diagonal, 0)

    @pl.when(alone & (core == 0))
    def _():
        mate_copy().wait_recv()

        def against(block, _):
            first = pl.multiple_of(block * 2 * LANES, 2 * LANES)
            scores = dot(own[...], mate[pl.ds(first, 2 * LANES), :])
            best = row_own[...]
            for j in range(2):
                same = id_own[...] == ids_of(me + 1, block * 2 + j)
                part = jnp.where(same, scores[:, j * LANES:(j + 1) * LANES], -1.0)
                best = jnp.maximum(best, part)
                mate_best[pl.ds(block * 2 + j, 1), :] = jnp.max(part, axis=0, keepdims=True)
            row_own[...] = best
            return 0

        lax.fori_loop(0, ROWS // (2 * LANES), against, 0)
        mate_answer().start()

    def settle(step, kind, rows):
        at = place(step, kind, slice(0, 1))
        columns[at] = jnp.maximum(columns[at], turned(rows))

    def older(step):
        right = gathered[0:step, NEAR * CHUNK:EXTRA * CHUNK, :].reshape(step * 2 * CHUNK, WIDTH)
        scores = dot(gathered[step, FAR * CHUNK:NEAR * CHUNK, :], right)
        pairs = [(s, kind) for s in range(step) for kind in (NEAR, SWAP)]
        best = fold(
            scores, id_rows[step, FAR * CHUNK:NEAR * CHUNK, :],
            [lanes_of(s, kind) for s, kind in pairs], None, pairs,
        )
        settle(step, FAR, best)

    def older_both(step):
        right = gathered[0:step, FAR * CHUNK:, :].reshape(step * 4 * CHUNK, WIDTH)
        scores = dot(gathered[step, 0:NEAR * CHUNK, :], right)
        base_ids = id_rows[step, 0:CHUNK, :]
        far_ids = id_rows[step, CHUNK:2 * CHUNK, :]
        rows = slice(step * CHUNK, (step + 1) * CHUNK)
        best_base, best_far = row_base[rows, :], jnp.full((CHUNK, LANES), -1.0, jnp.float32)
        for j, (s, kind) in enumerate((s, kind) for s in range(step) for kind in range(1, 5)):
            lanes = lanes_of(s, kind)
            part = jnp.where(base_ids == lanes, scores[0:CHUNK, j * LANES:(j + 1) * LANES], -1.0)
            best_base = jnp.maximum(best_base, part)
            if kind in (NEAR, SWAP):
                more = jnp.where(
                    far_ids == lanes, scores[CHUNK:, j * LANES:(j + 1) * LANES], -1.0
                )
                best_far = jnp.maximum(best_far, more)
                part = jnp.maximum(part, more)
            raise_to((s, kind), part)
        row_base[rows, :] = best_base
        settle(step, FAR, best_far)

    def newer(step):
        right = gathered[0:step + 1, FAR * CHUNK:NEAR * CHUNK, :].reshape((step + 1) * CHUNK, WIDTH)
        scores = dot(gathered[step, NEAR * CHUNK:EXTRA * CHUNK, :], right)
        pairs = [(s, FAR) for s in range(step + 1)]
        best = fold(
            scores, id_rows[step, NEAR * CHUNK:EXTRA * CHUNK, :],
            [lanes_of(s, kind) for s, kind in pairs], None, pairs,
        )
        settle(step, NEAR, best[0:CHUNK, :])
        settle(step, SWAP, best[CHUNK:, :])

    kinds = range(1, 5)

    def base_newer(step):
        count = (step + 1) * CHUNK
        left = gathered[0:step + 1, 0:CHUNK, :].reshape(count, WIDTH)
        ids = id_rows[0:step + 1, 0:CHUNK, :].reshape(count, LANES)
        row_base[0:count, :] = fold(
            dot(left, gathered[step, FAR * CHUNK:, :]), ids,
            [lanes_of(step, kind) for kind in kinds], row_base[0:count, :],
            [(step, kind) for kind in kinds],
        )

    def advance(step, _):
        near_copy(step).wait_recv()
        swap_copy(step).start()

        @pl.when(distant)
        def _():
            swap_copy(step).wait_recv()
            scores = dot(own[...], gathered[step, NEAR * CHUNK:EXTRA * CHUNK, :])
            row_base[...] = fold(
                scores, id_own[...], [lanes_of(step, kind) for kind in (NEAR, SWAP)],
                row_base[...], [(step, kind) for kind in (NEAR, SWAP)],
            )

        @pl.when(has_far)
        def _():
            far_copy(step).wait_recv()
            pl.when(core == 0)(lambda: extra_far(step).start())

        @pl.when(has_base)
        def _():
            base_copy(step).wait_recv()
            pl.when(core == 1)(lambda: extra_base(step).start())

        for known in range(1, STEPS):
            pl.when((step == known) & (x < 3))(functools.partial(older, known))
            pl.when((step == known) & last)(functools.partial(older_both, known))
        pl.when(has_extra)(lambda: extra_own(step).wait_recv())
        pl.when(jnp.logical_not(distant))(lambda: swap_copy(step).wait_recv())

        @pl.when(distant)
        def _():
            right = jnp.concatenate(
                [gathered[step, FAR * CHUNK:NEAR * CHUNK, :], gathered[step, EXTRA * CHUNK:, :]],
                axis=0,
            )
            row_base[...] = fold(
                dot(own[...], right), id_own[...],
                [lanes_of(step, kind) for kind in (FAR, EXTRA)],
                row_base[...], [(step, kind) for kind in (FAR, EXTRA)],
            )

        @pl.when((x < 3) & jnp.logical_not(distant))
        def _():
            scores = dot(own[...], gathered[step, FAR * CHUNK:, :])
            row_base[...] = fold(
                scores, id_own[...], [lanes_of(step, kind) for kind in kinds], row_base[...],
                [(step, kind) for kind in kinds],
            )

        for known in range(STEPS):
            pl.when((step == known) & last)(functools.partial(base_newer, known))
            pl.when(step == known)(functools.partial(newer, known))
        return 0

    lax.fori_loop(0, STEPS, advance, 0)

    best = jnp.max(columns[...], axis=1)
    for kind in kinds:
        reply[kind] = best[:, (kind - 1) * LANES:kind * LANES]

    def answer(kind, target):
        return remote(
            reply.at[kind], heard.at[kind], reply_s.at[kind], reply_r.at[kind], target
        )

    def flat(ref):
        return jnp.concatenate([turned(ref[chunk_rows(g), :]) for g in range(STEPS)], axis=0)

    pl.when(has_far)(lambda: answer(FAR, device(to_far, core)).start())
    answer(NEAR, device(to_near, core)).start()
    answer(SWAP, device(to_near, 1 - core)).start()
    pl.when((core == 0) & sends_back)(lambda: answer(EXTRA, device(to_base, 1)).start())
    pl.when((core == 1) & sends_back)(lambda: answer(EXTRA, device(to_far, 0)).start())
    based = flat(row_base)
    reply[BASE] = based
    best = flat(row_own)
    pl.when(has_base)(lambda: answer(BASE, device(-4, core)).start())
    nothing = jnp.full((STEPS, LANES), -1.0, jnp.float32)

    def hear(kind, comes, instead):
        @pl.when(comes)
        def _():
            answer(kind, partner).wait_recv()

        @pl.when(jnp.logical_not(comes))
        def _():
            heard[kind] = instead

    hear(BASE, sends_base, jnp.where(last, nothing, based))
    hear(FAR, sends_far, nothing)
    hear(EXTRA, (core == 1) | sends_far, nothing)
    answer(NEAR, partner).wait_recv()
    answer(SWAP, partner).wait_recv()
    for kind in range(5):
        best = jnp.maximum(best, heard[kind])
    out[...] = best

    def drain(step, _):
        near_copy(step).wait_send()
        pl.when(sends_far)(lambda: far_copy(step).wait_send())
        swap_copy(step).wait_send()
        pl.when(sends_extra)(lambda: extra_own(step).wait_send())

        pl.when(sends_base)(lambda: base_copy(step).wait_send())
        return 0

    lax.fori_loop(0, STEPS, drain, 0)
    answer(NEAR, partner).wait_send()
    answer(SWAP, partner).wait_send()
    pl.when(has_far)(lambda: answer(FAR, partner).wait_send())
    pl.when(has_base)(lambda: answer(BASE, partner).wait_send())
    pl.when(sends_back)(lambda: answer(EXTRA, partner).wait_send())
    pl.when(alone & (core == 1))(lambda: mate_copy().wait_send())
    pl.when(alone & (core == 0))(lambda: mate_answer().wait_send())


def shards(embeddings, offsets):
    block = pltpu.VMEM((ROWS, WIDTH), jnp.bfloat16)
    wide = pltpu.VMEM((ROWS, LANES), jnp.float32)
    steps = pltpu.SemaphoreType.DMA((STEPS,))
    best = pl.pallas_call(
        kernel,
        out_shape=jax.ShapeDtypeStruct((STEPS, LANES), jnp.float32),
        in_specs=[
            pl.BlockSpec(memory_space=pl.ANY),
            pl.BlockSpec(memory_space=pltpu.HBM),
        ],
        out_specs=pl.BlockSpec(memory_space=pltpu.VMEM),
        scratch_shapes=[
            block, block, block,
            pltpu.VMEM((STEPS, 5 * CHUNK, WIDTH), jnp.bfloat16),
            pltpu.SMEM((257,), jnp.int32),
            wide,
            pltpu.VMEM((STEPS, 4 * LANES, LANES), jnp.float32),
            pltpu.VMEM((STEPS, 1, LANES), jnp.float32),
            pltpu.VMEM((STEPS, 1, 4 * LANES), jnp.float32),
            pltpu.VMEM((2 * LANES, LANES), jnp.int32),
            wide, wide,
            pltpu.VMEM((STEPS, 8, 4 * LANES), jnp.float32),
            pltpu.VMEM((5, STEPS, LANES), jnp.float32),
            pltpu.VMEM((5, STEPS, LANES), jnp.float32),
            pltpu.VMEM((STEPS, LANES), jnp.float32),
            steps, pltpu.SemaphoreType.DMA(()),
            steps, steps, steps, steps, steps, pltpu.SemaphoreType.DMA((5,)),
            steps, steps, steps, steps, steps, pltpu.SemaphoreType.DMA((5,)),
            pltpu.SemaphoreType.DMA((3,)),
        ],
        compiler_params=pltpu.CompilerParams(
            collective_id=0, has_side_effects=True, vmem_limit_bytes=53 * 1024 * 1024
        ),
        name="match",
    )(embeddings, pltpu.with_memory_space_constraint(offsets, pltpu.HBM))
    return best.reshape(-1)


def solution(mesh):
    return jax.shard_map(
        shards,
        mesh=mesh,
        in_specs=(P(AXES, None), P()),
        out_specs=P(AXES),
        check_vma=False,
    )
```
